512 devices in a mesh: head: 8 (over y_lo, x), seq: 64 (over y_hi, z, core).
Axes of the slice: x: 4, y: 8 (y_hi: 4, y_lo: 2; y = y_hi * 2 + y_lo), z: 8, core: 2. Of those that a mesh axis runs over, the one named last changes fastest.
Arguments:
- queries: bfloat16 [2, 4096, 4096], P(None, 'seq', 'head'), may hold values from -256 to 256
- keys: bfloat16 [2, 4096, 4096], P(None, 'seq', 'head'), may hold values from -256 to 256
- values: bfloat16 [2, 4096, 4096], P(None, 'seq', 'head'), may hold values from -6 to 6
- token_rates: float32 [1, 16, 4096], P(None, 'head', 'seq'), may hold values from 0.1 to 1
- step_size: float32 [16], P('head'), may hold values from 0.3 to 1
- w_gate: bfloat16 [16, 256, 512], P('head', 'seq'), may hold values from -0.375 to 0.375
- w_up: bfloat16 [16, 256, 512], P('head', 'seq'), may hold values from -0.375 to 0.375
- w_down: bfloat16 [16, 512, 256], P('head', 'seq'), may hold values from -0.25 to 0.25
- norm_gain: float32 [4096], replicated, may hold values from 0.5 to 1.5
Outputs:
- mixed: bfloat16 [2, 4096, 4096], P(None, ('seq', 'head'))
The draws below stay inside these ranges and needn't reach their ends.
All inputs are finite; a program needn't handle non-finite values.
Results may differ from the reference program's by a relative error of at most 0.0095.
Values may be sent and summed in bfloat16 or wider, within the bound.
No kernel may reach another device: no remote copies, remote signals or barrier semaphores. Data moves between devices by JAX's collectives and lax.ppermute only.
A program may use at most 64 MiB of HBM per device.

```python
import math
import jax
import jax.numpy as jnp
from jax import lax

HEADS = 16
DH = 256
DF = 512
D = 4096
BLOCK = 4096
BLOCKS = 2
WIN = 512
NS_STEPS = 5


def pair_draw(key):
    base = jax.random.fold_in(key, 4242)
    key_query, key_key = jax.random.split(base, 2)
    shape = (BLOCKS, BLOCK, HEADS, DH)
    queries = 1.3 * jax.random.normal(key_query, shape, jnp.float32)
    keys = 1.3 * jax.random.normal(key_key, shape, jnp.float32)
    flat = (BLOCKS, BLOCK, HEADS * DH)
    return (jnp.clip(queries, -256.0, 256.0).reshape(flat), jnp.clip(keys, -256.0, 256.0).reshape(flat))


def draw_queries(key, part):
    return pair_draw(key)[0].astype(jnp.bfloat16)


def draw_keys(key, part):
    return pair_draw(key)[1].astype(jnp.bfloat16)


def shard_levels(own_key, dims, cuts, low, high):
    def one(dim, parts):
        draws = jax.random.uniform(jax.random.fold_in(jax.random.fold_in(own_key, 6), dim), (parts,), jnp.float32, low / len(cuts), high / len(cuts))
        return jnp.repeat(jnp.exp(draws), dims[dim] // parts).reshape((-1,) + (1,) * (len(dims) - dim - 1))

    loudness = one(*cuts[0])
    for cut in cuts[1:]:
        loudness = loudness * one(*cut)
    return loudness


def gaussian(stream_key, shape, spread, limit, pieces=(), kind=jnp.bfloat16):
    factor_of = shard_levels(stream_key, shape, pieces, -0.22, 0.18) if pieces else 1.0
    result = jax.random.normal(stream_key, shape, jnp.float32) * spread * factor_of
    return jnp.minimum(jnp.maximum(result, -limit), limit).astype(kind)


def setup_inputs(seed: int = 0) -> dict:
    streams_of = jax.random.split(jax.random.key(seed), 10)
    queries = draw_queries(jax.random.fold_in(streams_of[9], 71), 0)
    keys = draw_keys(jax.random.fold_in(streams_of[9], 71), 0)
    values = gaussian(streams_of[2], (BLOCKS, BLOCK, D), 1.0, 6.0, ((1, 64), (2, 8)))
    token_rates = jnp.clip(jnp.exp(math.log(1.0) - 2.3025851 * jax.random.uniform(streams_of[3], (BLOCKS - 1, HEADS, BLOCK), jnp.float32) ** shard_levels(streams_of[3], (BLOCKS - 1, HEADS, BLOCK), ((1, 8), (2, 64)), -0.2, 0.2)), 0.1, 1.0)
    step_size = jnp.clip(jnp.exp(math.log(1.0) - 1.2039728 * jax.random.uniform(streams_of[4], (HEADS,), jnp.float32) ** shard_levels(streams_of[4], (HEADS,), ((0, 8),), -0.2, 0.2)), 0.3, 1.0)
    w_gate = gaussian(streams_of[5], (HEADS, DH, DF), DH ** -0.5, 0.375, ((0, 8), (1, 64)))
    w_up = gaussian(streams_of[6], (HEADS, DH, DF), DH ** -0.5, 0.375, ((0, 8), (1, 64)))
    w_down = gaussian(streams_of[7], (HEADS, DF, DH), DF ** -0.5, 0.25, ((0, 8), (1, 64)))
    norm_gain = jnp.clip(1.0 + 0.1 * jax.random.normal(streams_of[8], (D,), jnp.float32), 0.5, 1.5)
    return dict(queries=queries, keys=keys, values=values, token_rates=token_rates, step_size=step_size, w_gate=w_gate, w_up=w_up, w_down=w_down, norm_gain=norm_gain)


def rms_norm(values_in):
    wide = values_in.astype(jnp.float32)
    mean_square = lax.optimization_barrier(jnp.mean(wide * wide, axis=-1, keepdims=True))
    return (wide * lax.rsqrt(mean_square + 1e-06)).astype(jnp.bfloat16)

def newton(grad_in):
    norm_value = jnp.sqrt(jnp.sum(grad_in * grad_in))
    iterate = grad_in / (norm_value + 1e-07)
    for _ in range(NS_STEPS):
        gram = jnp.dot(iterate, iterate.T, precision=lax.Precision.HIGHEST, preferred_element_type=jnp.float32)
        poly = -4.775 * gram + 2.0315 * jnp.dot(gram, gram, precision=lax.Precision.HIGHEST, preferred_element_type=jnp.float32)
        iterate = 3.4445 * iterate + jnp.dot(poly, iterate, precision=lax.Precision.HIGHEST, preferred_element_type=jnp.float32)
    return iterate

def window_head(query_h, key_h, value_h):
    total_len = query_h.shape[0]
    tile = math.gcd(total_len, 512)
    padding = jnp.zeros((WIN, DH), key_h.dtype)
    key_pad = jnp.concatenate([padding, key_h], 0)
    value_pad = jnp.concatenate([padding, value_h], 0)
    scale = 1.0 / math.sqrt(DH)

    def one_tile(tile_index):
        start = (tile_index * tile).astype(jnp.int32)
        query_tile = lax.dynamic_slice_in_dim(query_h, start, tile, 0)
        key_tile = lax.dynamic_slice_in_dim(key_pad, start, tile + WIN, 0)
        value_tile = lax.dynamic_slice_in_dim(value_pad, start, tile + WIN, 0)
        scores = jnp.dot(query_tile, key_tile.T, preferred_element_type=jnp.float32) * scale
        query_pos = start + jnp.arange(tile, dtype=jnp.int32)
        key_pos = start - WIN + jnp.arange(tile + WIN, dtype=jnp.int32)
        row_gap = query_pos[:, None] - key_pos[None, :]
        allowed = (row_gap >= 0) & (row_gap < WIN) & (key_pos[None, :] >= 0)
        scores = jnp.where(allowed, scores, -1e+30)
        row_top = lax.optimization_barrier(jnp.max(scores, axis=-1, keepdims=True))
        exp_scores = jnp.exp(scores - row_top)
        attn_weights = (exp_scores / lax.optimization_barrier(jnp.sum(exp_scores, axis=-1, keepdims=True))).astype(jnp.bfloat16)
        return jnp.dot(attn_weights, value_tile, preferred_element_type=jnp.float32)
    tiles = lax.map(one_tile, jnp.arange(total_len // tile, dtype=jnp.int32))
    return tiles.reshape(total_len, DH)

def fast_head(query_h, key_h, value_h, rates_h, step_h, gate_fast, up_fast, down_fast):
    outputs = []
    for block_index in range(BLOCKS):
        query_norm = rms_norm(query_h[block_index])
        gate_query = jnp.dot(query_norm, gate_fast, preferred_element_type=jnp.float32)
        up_query = jnp.dot(query_norm, up_fast, preferred_element_type=jnp.float32)
        hidden = (jax.nn.silu(gate_query) * up_query).astype(jnp.bfloat16)
        outputs.append(jnp.dot(hidden, down_fast, preferred_element_type=jnp.float32))
        if block_index < BLOCKS - 1:
            keys_now = rms_norm(key_h[block_index])
            vals_now = value_h[block_index]
            gate_pre = jnp.dot(keys_now, gate_fast, preferred_element_type=jnp.float32)
            up_pre = jnp.dot(keys_now, up_fast, preferred_element_type=jnp.float32)
            back = jnp.dot(vals_now, down_fast.T, preferred_element_type=jnp.float32)
            rate_col = rates_h[block_index][:, None]
            sigmoid_val = jax.nn.sigmoid(gate_pre)
            act_val = gate_pre * sigmoid_val
            d_gate = (rate_col * back * up_pre * sigmoid_val * (1.0 + gate_pre * (1.0 - sigmoid_val))).astype(jnp.bfloat16)
            d_up = (rate_col * back * act_val).astype(jnp.bfloat16)
            h_rate = (rate_col * act_val * up_pre).astype(jnp.bfloat16)
            grad_gate = jnp.dot(keys_now.T, d_gate, preferred_element_type=jnp.float32)
            grad_up = jnp.dot(keys_now.T, d_up, preferred_element_type=jnp.float32)
            grad_down_t = jnp.dot(vals_now.T, h_rate, preferred_element_type=jnp.float32)
            gate_fast = (gate_fast.astype(jnp.float32) + step_h * newton(grad_gate)).astype(jnp.bfloat16)
            up_fast = (up_fast.astype(jnp.float32) + step_h * newton(grad_up)).astype(jnp.bfloat16)
            down_fast = (down_fast.astype(jnp.float32) + step_h * newton(grad_down_t).T).astype(jnp.bfloat16)
    return jnp.stack(outputs)

def reference(queries, keys, values, token_rates, step_size, w_gate, w_up, w_down, norm_gain):
    total_len = BLOCKS * BLOCK

    def per_head(head_index):
        column = (head_index * DH).astype(jnp.int32)
        query_h = lax.dynamic_slice_in_dim(queries, column, DH, 2)
        key_h = lax.dynamic_slice_in_dim(keys, column, DH, 2)
        value_h = lax.dynamic_slice_in_dim(values, column, DH, 2)
        attention = window_head(query_h.reshape(total_len, DH), key_h.reshape(total_len, DH), value_h.reshape(total_len, DH))
        attention = attention.reshape(BLOCKS, BLOCK, DH)
        fast_out = fast_head(query_h, key_h, value_h, token_rates[:, head_index], step_size[head_index], w_gate[head_index], w_up[head_index], w_down[head_index])
        return (fast_out + attention).astype(jnp.bfloat16)
    combined = lax.map(per_head, jnp.arange(HEADS, dtype=jnp.int32))
    combined = jnp.transpose(combined, (1, 2, 0, 3)).reshape(BLOCKS, BLOCK, D)
    wide = combined.astype(jnp.float32)
    mean_square = lax.optimization_barrier(jnp.mean(wide * wide, axis=-1, keepdims=True))
    return (wide * lax.rsqrt(mean_square + 1e-06) * norm_gain).astype(jnp.bfloat16)
```

```python
import math

import jax
import jax.numpy as jnp
from jax import lax
from jax.experimental import pallas as pl
from jax.experimental.pallas import tpu as pltpu
from jax.sharding import Mesh
from jax.sharding import PartitionSpec as P

DH = 256
DF = 512
NS_STEPS = 5
CHIPS = 32
TOK = 128
REACH = 4
RING = ("y_hi", "z")
F32 = jnp.float32
BF = jnp.bfloat16


def matmul(left, right):
    return lax.dot_general(left, right, (((1,), (0,)), ((), ())), preferred_element_type=F32)


def matmul_nt(left, right):
    return lax.dot_general(left, right, (((1,), (1,)), ((), ())), preferred_element_type=F32)


def matmul_tn(left, right):
    return lax.dot_general(left, right, (((0,), (0,)), ((), ())), preferred_element_type=F32)


def halves(wide):
    high = wide.astype(BF)
    return high, (wide - high.astype(F32)).astype(BF)


def rms_norm(values_in):
    wide = values_in.astype(F32)
    mean_square = jnp.mean(wide * wide, axis=-1, keepdims=True)
    return (wide * lax.rsqrt(mean_square + 1e-06)).astype(BF)


def sigmoid(value):
    return 1.0 / (1.0 + jnp.exp(-value))


def rows_of(ref, first, count, width):
    piece = ref[:, first : first + 8, :].astype(F32)
    return piece.reshape(count * 8, width).astype(BF)


def fast_forward(query, gate_fast, up_fast, down_fast):
    query_norm = rms_norm(query)
    gate_query = matmul(query_norm, gate_fast)
    up_query = matmul(query_norm, up_fast)
    hidden = (gate_query * sigmoid(gate_query) * up_query).astype(BF)
    return matmul(hidden, down_fast)


def grad_kernel(kv_ref, rate_ref, raw_ref, grad_ref, gate_ref, up_ref, down_ref):
    out_row = lax.broadcasted_iota(jnp.int32, (DH, 2 * DH), 0)
    in_row = lax.broadcasted_iota(jnp.int32, (DH, 2 * DH), 1)
    for first, target in ((0, gate_ref), (8, up_ref)):
        mixed = rows_of(raw_ref, first, 64, DH)
        for half in range(2):
            pick = (out_row // 4) * 8 + half * 4 + out_row % 4
            chosen = jnp.where(in_row == pick, 1.0, 0.0).astype(BF)
            target[:, half * DH : (half + 1) * DH] = matmul(chosen, mixed).astype(BF)
    down_ref[...] = rows_of(raw_ref, 16, 64, DH)
    keys_now = rms_norm(kv_ref[0, 0])
    vals_now = kv_ref[1, 0]
    row = lax.broadcasted_iota(jnp.int32, (TOK, TOK), 0)
    column = lax.broadcasted_iota(jnp.int32, (TOK, TOK), 1)
    spread = jnp.where(row == column, jnp.broadcast_to(rate_ref[...], (TOK, TOK)), 0.0)
    rate_col = jnp.sum(spread, axis=1, keepdims=True)
    gate_pre = matmul(keys_now, gate_ref[...])
    up_pre = matmul(keys_now, up_ref[...])
    back = matmul_nt(vals_now, down_ref[...])
    sigmoid_val = sigmoid(gate_pre)
    act_val = gate_pre * sigmoid_val
    rate_back = rate_col * back
    d_gate = (rate_back * up_pre * sigmoid_val * (1.0 + gate_pre * (1.0 - sigmoid_val))).astype(BF)
    d_up = (rate_back * act_val).astype(BF)
    h_rate = (rate_col * act_val * up_pre).astype(BF)
    for index, (left, right) in enumerate(
        ((keys_now, d_gate), (keys_now, d_up), (vals_now, h_rate))
    ):
        grad = matmul_tn(left, right).reshape(CHIPS, 8, DF)
        grad_ref[:, index * 8 : index * 8 + 8, :] = grad.astype(BF)


def sum_kernel(parts_ref, total_ref):
    total = jnp.sum(parts_ref[...].astype(F32), axis=0, keepdims=True)
    total_ref[...] = jnp.broadcast_to(total, (CHIPS, 24, DF)).astype(BF)


def attention_kernel(
    chip_ref, q_ref, own_ref, c1_ref, c2_ref, c3_ref, c4_ref, gate_ref, up_ref, down_ref, out_ref
):
    chip = chip_ref[0]
    row = lax.broadcasted_iota(jnp.int32, (TOK, TOK), 0)
    column = lax.broadcasted_iota(jnp.int32, (TOK, TOK), 1)
    scale = 1.0 / math.sqrt(DH)
    chunks = (own_ref, c1_ref, c2_ref, c3_ref, c4_ref)
    for block in range(2):
        query = q_ref[block]
        scores = []
        for distance, chunk in enumerate(chunks):
            behind = (chip < distance).astype(jnp.int32)
            slot = jnp.maximum(block - behind, 0)
            score = matmul_nt(query, chunk[0, slot]) * scale
            if distance == 0:
                score = jnp.where(row >= column, score, -1e30)
            elif distance == REACH:
                score = jnp.where(row < column, score, -1e30)
            if block == 0 and distance > 0:
                score = jnp.where(behind + jnp.zeros_like(row) > 0, -1e30, score)
            scores.append(score)
        top = scores[0]
        for score in scores[1:]:
            top = jnp.maximum(top, score)
        row_top = jnp.max(top, axis=-1, keepdims=True)
        exps = [jnp.exp(score - row_top) for score in scores]
        total = exps[0]
        for exp_score in exps[1:]:
            total = total + exp_score
        row_sum = jnp.sum(total, axis=-1, keepdims=True)
        result = None
        for distance, chunk in enumerate(chunks):
            behind = (chip < distance).astype(jnp.int32)
            slot = jnp.maximum(block - behind, 0)
            weights = (exps[distance] / row_sum).astype(BF)
            part = matmul(weights, chunk[1, slot])
            result = part if result is None else result + part
        if block == 0:
            result = result + fast_forward(query, gate_ref[...], up_ref[...], down_ref[...])
        out_ref[block] = result


def newton_kernel(
    step_ref, total_ref, gate_ref, up_ref, down_ref, q_ref, base_ref, out_ref, iterate_ref
):
    for index in range(3):
        piece = total_ref[:, index * 8 : index * 8 + 8, :].astype(F32)
        grad = piece.reshape(DH, DF)
        square = jnp.sum(jnp.sum(grad * grad, axis=0, keepdims=True), axis=1, keepdims=True)
        iterate_ref[index] = grad / (jnp.sqrt(square) + 1e-07)

    def one_step(_, carry):
        for index in range(3):
            iterate = iterate_ref[index]
            high, low = halves(iterate)
            gram = matmul_nt(high, high) + (matmul_nt(high, low) + matmul_nt(low, high))
            gram_high, gram_low = halves(gram)
            square = matmul(gram_high, gram_high) + (
                matmul(gram_high, gram_low) + matmul(gram_low, gram_high)
            )
            poly_high, poly_low = halves(-4.775 * gram + 2.0315 * square)
            iterate_ref[index] = 3.4445 * iterate + (
                matmul(poly_high, high) + (matmul(poly_high, low) + matmul(poly_low, high))
            )
        return carry

    lax.fori_loop(0, NS_STEPS, one_step, 0)
    step = step_ref[0]
    gate_fast = (gate_ref[...].astype(F32) + step * iterate_ref[0]).astype(BF)
    up_fast = (up_ref[...].astype(F32) + step * iterate_ref[1]).astype(BF)
    down_fast = (down_ref[...].astype(F32) + step * iterate_ref[2].T).astype(BF)
    fast = fast_forward(q_ref[1], gate_fast, up_fast, down_fast)
    out_ref[:, 0] = base_ref[0].reshape(16, 8, DH).astype(BF)
    out_ref[:, 1] = (fast + base_ref[1]).reshape(16, 8, DH).astype(BF)


def norm_kernel(parts_ref, gain_ref, out_ref):
    square = None
    for source in range(16):
        wide = parts_ref[source].astype(F32)
        part = jnp.sum(wide * wide, axis=-1, keepdims=True)
        square = part if square is None else square + part
    scale = lax.rsqrt(square * (1.0 / (16 * DH)) + 1e-06)
    for source in range(16):
        head = 2 * (source % 8) + source // 8
        columns = slice(head * DH, (head + 1) * DH)
        wide = parts_ref[source].astype(F32) * scale * gain_ref[:, columns][None]
        out_ref[:, :, columns] = wide.astype(BF)


PARAMS = pltpu.CompilerParams(vmem_limit_bytes=16 * 1024 * 1024)
VMEM = pl.BlockSpec(memory_space=pltpu.VMEM)
SMEM = pl.BlockSpec(memory_space=pltpu.SMEM)


def body(queries, keys, values, token_rates, step_size, w_gate, w_up, w_down, norm_gain):
    core = lax.axis_index("core")
    chip = lax.axis_index(RING)
    raw = jnp.concatenate(
        [
            w_gate.reshape(2, 4, 2, DH).transpose(0, 2, 1, 3).reshape(2, 8, DH),
            w_up.reshape(2, 4, 2, DH).transpose(0, 2, 1, 3).reshape(2, 8, DH),
            w_down,
        ],
        1,
    )
    raw = jnp.broadcast_to(raw[None], (CHIPS, 2, 24, DH)).reshape(64, 24, DH)
    raw = lax.all_to_all(raw, RING + ("core",), 0, 0, tiled=True)

    tokens = jnp.stack([queries, keys, values]).reshape(3, 2, 64, 2, DH)
    tokens = tokens.transpose(3, 0, 1, 2, 4).reshape(2, 384, DH)
    first = token_rates[0].astype(BF)
    rest = token_rates[0] - first.astype(F32)
    second = rest.astype(BF)
    third = (rest - second.astype(F32)).astype(BF)
    rates = jnp.concatenate([first, second, third, jnp.zeros_like(first)], 1)
    rates = jnp.pad(rates[:, None, :], ((0, 0), (0, 7), (0, 0)))
    mine = lax.all_to_all(jnp.concatenate([tokens, rates], 1), "core", 0, 0, tiled=True)
    tokens = mine[:, :384].reshape(2, 3, 2, 64, DH).transpose(1, 2, 0, 3, 4)
    tokens = tokens.reshape(3, 2, TOK, DH)
    query, own = tokens[0], tokens[1:]
    rates = mine[:, 384, :192].astype(F32).reshape(2, 3, 64)
    rates = (rates[:, 0] + (rates[:, 1] + rates[:, 2])).reshape(1, TOK)

    grad, gate_fast, up_fast, down_fast = pl.pallas_call(
        grad_kernel,
        out_shape=(
            jax.ShapeDtypeStruct((CHIPS, 24, DF), BF),
            jax.ShapeDtypeStruct((DH, DF), BF),
            jax.ShapeDtypeStruct((DH, DF), BF),
            jax.ShapeDtypeStruct((DF, DH), BF),
        ),
        in_specs=[VMEM] * 3,
        out_specs=(VMEM,) * 4,
        compiler_params=PARAMS,
        name="grad",
    )(own, rates, raw)
    parts = lax.all_to_all(grad, RING, 0, 0, tiled=True)
    total = pl.pallas_call(
        sum_kernel,
        out_shape=jax.ShapeDtypeStruct((CHIPS, 24, DF), BF),
        in_specs=[VMEM],
        out_specs=VMEM,
        compiler_params=PARAMS,
        name="sum",
    )(parts)
    total = lax.all_to_all(total, RING, 0, 0, tiled=True)

    chunks = [own]
    for _ in range(REACH):
        ring = [(i, (i + 1) % CHIPS) for i in range(CHIPS)]
        chunks.append(lax.ppermute(chunks[-1], RING, ring))
    base = pl.pallas_call(
        attention_kernel,
        out_shape=jax.ShapeDtypeStruct((2, TOK, DH), F32),
        in_specs=[SMEM] + [VMEM] * 9,
        out_specs=VMEM,
        compiler_params=PARAMS,
        name="window",
    )(chip.astype(jnp.int32).reshape(1), query, *chunks, gate_fast, up_fast, down_fast)

    step = lax.dynamic_slice_in_dim(step_size, core, 1, 0)
    combined = pl.pallas_call(
        newton_kernel,
        out_shape=jax.ShapeDtypeStruct((16, 2, 8, DH), BF),
        in_specs=[SMEM] + [VMEM] * 6,
        out_specs=VMEM,
        scratch_shapes=[pltpu.VMEM((3, DH, DF), F32)],
        compiler_params=PARAMS,
        name="newton",
    )(step, total, gate_fast, up_fast, down_fast, query, base)
    gathered = lax.all_to_all(combined, ("core", "y_lo", "x"), 0, 0, tiled=True)
    return pl.pallas_call(
        norm_kernel,
        out_shape=jax.ShapeDtypeStruct((2, 8, 16 * DH), BF),
        in_specs=[VMEM] * 2,
        out_specs=VMEM,
        compiler_params=PARAMS,
        name="norm",
    )(gathered, norm_gain.reshape(1, 16 * DH))


def solution(mesh):
    fine = Mesh(mesh.devices.reshape(2, 4, 4, 8, 2), ("y_lo", "x", "y_hi", "z", "core"))
    seq = RING + ("core",)
    head = ("y_lo", "x")
    placed = (
        P(None, seq, head),
        P(None, seq, head),
        P(None, seq, head),
        P(None, head, seq),
        P(head),
        P(head, seq, None),
        P(head, seq, None),
        P(head, seq, None),
        P(),
    )
    return jax.shard_map(
        body, mesh=fine, in_specs=placed, out_specs=P(None, seq + head, None), check_vma=False
    )
```

```python
import math

import jax
import jax.numpy as jnp
from jax import lax
from jax.experimental import pallas as pl
from jax.experimental.pallas import tpu as pltpu
from jax.sharding import Mesh
from jax.sharding import PartitionSpec as P

DH = 256
DF = 512
PART = 128
NS_STEPS = 5
CHIPS = 32
TOK = 128
REACH = 4
RING = ("y_hi", "z")
F32 = jnp.float32
BF = jnp.bfloat16


def matmul(left, right):
    return lax.dot_general(left, right, (((1,), (0,)), ((), ())), preferred_element_type=F32)


def matmul_nt(left, right):
    return lax.dot_general(left, right, (((1,), (1,)), ((), ())), preferred_element_type=F32)


def matmul_tn(left, right):
    return lax.dot_general(left, right, (((0,), (0,)), ((), ())), preferred_element_type=F32)


def halves(wide):
    high = wide.astype(BF)
    return high, (wide - high.astype(F32)).astype(BF)


def rms_norm(values_in):
    wide = values_in.astype(F32)
    mean_square = jnp.mean(wide * wide, axis=-1, keepdims=True)
    return (wide * lax.rsqrt(mean_square + 1e-06)).astype(BF)


def sigmoid(value):
    return 1.0 / (1.0 + jnp.exp(-value))


def fast_forward(query, gate_fast, up_fast, down_fast):
    query_norm = rms_norm(query)
    gate_query = matmul(query_norm, gate_fast)
    up_query = matmul(query_norm, up_fast)
    hidden = (gate_query * sigmoid(gate_query) * up_query).astype(BF)
    return matmul(hidden, down_fast)


def pack_kernel(
    q_ref, k_ref, v_ref, rate_ref, gate_ref, up_ref, down_ref, swap_ref, pool_ref, weight_ref
):
    for head in range(2):
        columns = slice(head * DH, (head + 1) * DH)
        for index, ref in enumerate((q_ref, k_ref, v_ref)):
            for block in range(2):
                first = (index * 2 + block) * 64
                swap_ref[head, first : first + 64, :] = ref[block, :, columns]
        rate = rate_ref[0, head : head + 1, :]
        high = rate.astype(BF).astype(F32)
        middle = (rate - high).astype(BF).astype(F32)
        low = (rate - high) - middle
        terms = jnp.concatenate([high, middle, low, jnp.zeros_like(rate)], 1)
        terms = jnp.broadcast_to(terms, (8, DH)).astype(BF)
        low_half = down_ref[head, :, :128]
        high_half = down_ref[head, :, 128:]
        for row in range(4):
            target = row * 2 + head
            pool_ref[target, 0:64, :] = k_ref[0, :, columns]
            pool_ref[target, 64:128, :] = v_ref[0, :, columns]
            pool_ref[target, 128:136, :] = terms
            part = slice(row * PART, (row + 1) * PART)
            pair = [gate_ref[head, :, part].astype(F32), up_ref[head, :, part].astype(F32)]
            pair = jnp.concatenate(pair, 0).astype(BF)
            for depth in range(8):
                target = (row * 8 + depth) * 2 + head
                weight_ref[target, 0:8, :] = pair
                weight_ref[target, 8:16, :] = low_half
                weight_ref[target, 16:24, :] = high_half


def grad_kernel(row_ref, pool_ref, raw_ref, _, grad_ref, slice_ref, down_ref):
    out_row = lax.broadcasted_iota(jnp.int32, (DH, 2 * DH), 0)
    in_row = lax.broadcasted_iota(jnp.int32, (DH, 2 * DH), 1)
    mixed = raw_ref[:, 0:8, :].astype(F32).reshape(2 * DH, PART).astype(BF)
    weights = []
    for index in range(2):
        pick = (out_row // 4) * 8 + index * 4 + out_row % 4
        chosen = jnp.where(in_row == pick, 1.0, 0.0).astype(BF)
        weights.append(matmul(chosen, mixed).astype(BF))
        for row in range(4):
            slice_ref[row, index * DH : (index + 1) * DH, :] = weights[index]
    for index in range(2):
        half = raw_ref[:, 8 + 8 * index : 16 + 8 * index, :].astype(F32)
        down_ref[:, index * 128 : (index + 1) * 128] = half.reshape(DF, 128).astype(BF)
    gate_part, up_part = weights
    down_part = down_ref[pl.ds(pl.multiple_of(row_ref[0] * PART, PART), PART), :]
    equal = lax.broadcasted_iota(jnp.int32, (64, 64), 0) == lax.broadcasted_iota(
        jnp.int32, (64, 64), 1
    )
    columns = []
    for source in range(8):
        terms = pool_ref[source, 128:136, :].astype(F32)[0:1]
        rate = terms[:, 0:64] + (terms[:, 64:128] + terms[:, 128:192])
        spread = jnp.where(equal, jnp.broadcast_to(rate, (64, 64)), 0.0)
        columns.append(jnp.sum(spread, axis=1, keepdims=True))
    rate_col = jnp.concatenate(columns, 0)
    keys_now = rms_norm(pool_ref[:, 0:64, :].reshape(4 * TOK, DH))
    vals_now = pool_ref[:, 64:128, :].reshape(4 * TOK, DH)
    gate_pre = matmul(keys_now, gate_part)
    up_pre = matmul(keys_now, up_part)
    back = matmul_nt(vals_now, down_part)
    sigmoid_val = sigmoid(gate_pre)
    act_val = gate_pre * sigmoid_val
    rate_back = rate_col * back
    d_gate = (rate_back * up_pre * sigmoid_val * (1.0 + gate_pre * (1.0 - sigmoid_val))).astype(BF)
    d_up = (rate_back * act_val).astype(BF)
    h_rate = (rate_col * act_val * up_pre).astype(BF)
    for index, (left, right) in enumerate(
        ((keys_now, d_gate), (keys_now, d_up), (vals_now, h_rate))
    ):
        grad = matmul_tn(left, right).reshape(8, 32, PART)
        grad_ref[:, index * 32 : index * 32 + 32, :] = grad.astype(BF)


def sum_kernel(parts_ref, _, __, total_ref):
    total = jnp.sum(parts_ref[...].astype(F32), axis=0, keepdims=True)
    total_ref[...] = jnp.broadcast_to(total, (8, 96, PART)).astype(BF)


def widen_kernel(piece_ref, _, total_ref):
    for row in range(4):
        total_ref[row] = piece_ref[...]


def whole_weights(slices_ref, index):
    rows = slice(index * DH, (index + 1) * DH)
    return jnp.concatenate([slices_ref[row, rows, :] for row in range(4)], 1)


def attention_kernel(
    chip_ref, own_ref, c1_ref, c2_ref, c3_ref, c4_ref, slices_ref, down_ref, out_ref
):
    chip = chip_ref[0]
    row = lax.broadcasted_iota(jnp.int32, (TOK, TOK), 0)
    column = lax.broadcasted_iota(jnp.int32, (TOK, TOK), 1)
    scale = 1.0 / math.sqrt(DH)
    chunks = (c1_ref, c2_ref, c3_ref, c4_ref)

    def rows_of(distance, index, block):
        if distance == 0:
            place = 2 + 2 * index + block
            return jnp.concatenate([own_ref[0, place], own_ref[1, place]], 0)
        behind = (chip < distance).astype(jnp.int32)
        place = 2 * index + jnp.maximum(block - behind, 0)
        chunk = chunks[distance - 1]
        return jnp.concatenate([chunk[0, place], chunk[1, place]], 0)

    for block in range(2):
        query = jnp.concatenate([own_ref[0, block], own_ref[1, block]], 0)
        scores = []
        for distance in range(REACH + 1):
            score = matmul_nt(query, rows_of(distance, 0, block)) * scale
            if distance == 0:
                score = jnp.where(row >= column, score, -1e30)
            elif distance == REACH:
                score = jnp.where(row < column, score, -1e30)
            if block == 0 and distance > 0:
                behind = (chip < distance).astype(jnp.int32)
                score = jnp.where(behind + jnp.zeros_like(row) > 0, -1e30, score)
            scores.append(score)
        top = scores[0]
        for score in scores[1:]:
            top = jnp.maximum(top, score)
        row_top = jnp.max(top, axis=-1, keepdims=True)
        exps = [jnp.exp(score - row_top) for score in scores]
        total = exps[0]
        for exp_score in exps[1:]:
            total = total + exp_score
        row_sum = jnp.sum(total, axis=-1, keepdims=True)
        result = None
        for distance in range(REACH + 1):
            weights = (exps[distance] / row_sum).astype(BF)
            part = matmul(weights, rows_of(distance, 1, block))
            result = part if result is None else result + part
        if block == 0:
            gate_fast, up_fast = whole_weights(slices_ref, 0), whole_weights(slices_ref, 1)
            result = result + fast_forward(query, gate_fast, up_fast, down_ref[...])
        out_ref[block] = result


def newton_kernel(
    step_ref, total_ref, slices_ref, down_ref, own_ref, base_ref, out_ref, iterate_ref
):
    for index in range(3):
        rows = slice(index * 32, index * 32 + 32)
        pieces = [total_ref[row, :, rows, :].astype(F32).reshape(DH, PART) for row in range(4)]
        grad = jnp.concatenate(pieces, 1)
        square = jnp.sum(jnp.sum(grad * grad, axis=0, keepdims=True), axis=1, keepdims=True)
        iterate_ref[index] = grad / (jnp.sqrt(square) + 1e-07)

    def one_step(_, carry):
        for index in range(3):
            iterate = iterate_ref[index]
            high, low = halves(iterate)
            gram = matmul_nt(high, high) + (matmul_nt(high, low) + matmul_nt(low, high))
            gram_high, gram_low = halves(gram)
            square = matmul(gram_high, gram_high) + (
                matmul(gram_high, gram_low) + matmul(gram_low, gram_high)
            )
            poly_high, poly_low = halves(-4.775 * gram + 2.0315 * square)
            iterate_ref[index] = 3.4445 * iterate + (
                matmul(poly_high, high) + (matmul(poly_high, low) + matmul(poly_low, high))
            )
        return carry

    lax.fori_loop(0, NS_STEPS, one_step, 0)
    step = step_ref[0]
    gate_fast = (whole_weights(slices_ref, 0).astype(F32) + step * iterate_ref[0]).astype(BF)
    up_fast = (whole_weights(slices_ref, 1).astype(F32) + step * iterate_ref[1]).astype(BF)
    down_fast = (down_ref[...].astype(F32) + step * iterate_ref[2].T).astype(BF)
    query = jnp.concatenate([own_ref[0, 1], own_ref[1, 1]], 0)
    fast = fast_forward(query, gate_fast, up_fast, down_fast)
    out_ref[:, 0] = base_ref[0].reshape(16, 8, DH).astype(BF)
    out_ref[:, 1] = (fast + base_ref[1]).reshape(16, 8, DH).astype(BF)


def norm_kernel(parts_ref, gain_ref, out_ref):
    square = None
    for source in range(16):
        wide = parts_ref[source].astype(F32)
        part = jnp.sum(wide * wide, axis=-1, keepdims=True)
        square = part if square is None else square + part
    scale = lax.rsqrt(square * (1.0 / (16 * DH)) + 1e-06)
    for source in range(16):
        head = 2 * (source % 8) + source // 8
        columns = slice(head * DH, (head + 1) * DH)
        wide = parts_ref[source].astype(F32) * scale * gain_ref[:, columns][None]
        out_ref[:, :, columns] = wide.astype(BF)


PARAMS = pltpu.CompilerParams(vmem_limit_bytes=16 * 1024 * 1024)
VMEM = pl.BlockSpec(memory_space=pltpu.VMEM)
ANY = pl.BlockSpec(memory_space=pl.ANY)
SMEM = pl.BlockSpec(memory_space=pltpu.SMEM)


def shape_of(shape, dtype=BF):
    return jax.ShapeDtypeStruct(shape, dtype)


def body(queries, keys, values, token_rates, step_size, w_gate, w_up, w_down, norm_gain):
    core = lax.axis_index("core")
    chip = lax.axis_index(RING).astype(jnp.int32).reshape(1)
    line = lax.axis_index("y_hi").astype(jnp.int32).reshape(1)
    swap, pool, raw = pl.pallas_call(
        pack_kernel,
        out_shape=(shape_of((2, 384, DH)), shape_of((8, 136, DH)), shape_of((64, 24, 128))),
        in_specs=[VMEM] * 7,
        out_specs=(VMEM,) * 3,
        compiler_params=PARAMS,
        name="pack",
    )(queries, keys, values, token_rates, w_gate, w_up, w_down)
    raw = lax.all_to_all(raw, RING + ("core",), 0, 0, tiled=True)
    pool = lax.all_to_all(pool, ("y_hi", "core"), 0, 0, tiled=True)
    own = lax.all_to_all(swap, "core", 0, 0, tiled=True)

    ring = [(i, (i + 1) % CHIPS) for i in range(CHIPS)]
    chunks = [lax.ppermute(own[:, 128:], RING, ring)]

    grad, slices, down_fast = pl.pallas_call(
        grad_kernel,
        out_shape=(shape_of((8, 96, PART)), shape_of((4, 2 * DH, PART)), shape_of((DF, DH))),
        in_specs=[SMEM] + [VMEM] * 2 + [ANY],
        out_specs=(VMEM,) * 3,
        compiler_params=PARAMS,
        name="grad",
    )(line, pool, raw, chunks[0])
    chunks.append(lax.ppermute(chunks[-1], RING, ring))
    parts = lax.all_to_all(grad, "z", 0, 0, tiled=True)
    slices = lax.all_to_all(slices, "y_hi", 0, 0, tiled=True)
    total = pl.pallas_call(
        sum_kernel,
        out_shape=shape_of((8, 96, PART)),
        in_specs=[VMEM, ANY, ANY],
        out_specs=VMEM,
        compiler_params=PARAMS,
        name="sum",
    )(parts, chunks[1], slices)
    chunks.append(lax.ppermute(chunks[-1], RING, ring))
    total = lax.all_to_all(total, "z", 0, 0, tiled=True)
    total = pl.pallas_call(
        widen_kernel,
        out_shape=shape_of((4, 8, 96, PART)),
        in_specs=[VMEM, ANY],
        out_specs=VMEM,
        compiler_params=PARAMS,
        name="widen",
    )(total, chunks[2])
    chunks.append(lax.ppermute(chunks[-1], RING, ring))
    total = lax.all_to_all(total, "y_hi", 0, 0, tiled=True)

    own = own.reshape(2, 6, 64, DH)
    chunks = [chunk.reshape(2, 4, 64, DH) for chunk in chunks]
    base = pl.pallas_call(
        attention_kernel,
        out_shape=shape_of((2, TOK, DH), F32),
        in_specs=[SMEM] + [VMEM] * 7,
        out_specs=VMEM,
        compiler_params=PARAMS,
        name="window",
    )(chip, own, *chunks, slices, down_fast)

    step = lax.dynamic_slice_in_dim(step_size, core, 1, 0)
    combined = pl.pallas_call(
        newton_kernel,
        out_shape=shape_of((16, 2, 8, DH)),
        in_specs=[SMEM] + [VMEM] * 5,
        out_specs=VMEM,
        scratch_shapes=[pltpu.VMEM((3, DH, DF), F32)],
        compiler_params=PARAMS,
        name="newton",
    )(step, total, slices, down_fast, own, base)
    gathered = lax.all_to_all(combined, ("core", "y_lo", "x"), 0, 0, tiled=True)
    return pl.pallas_call(
        norm_kernel,
        out_shape=jax.ShapeDtypeStruct((2, 8, 16 * DH), BF),
        in_specs=[VMEM] * 2,
        out_specs=VMEM,
        compiler_params=PARAMS,
        name="norm",
    )(gathered, norm_gain.reshape(1, 16 * DH))


def solution(mesh):
    fine = Mesh(mesh.devices.reshape(2, 4, 4, 8, 2), ("y_lo", "x", "y_hi", "z", "core"))
    seq = RING + ("core",)
    head = ("y_lo", "x")
    placed = (
        P(None, seq, head),
        P(None, seq, head),
        P(None, seq, head),
        P(None, head, seq),
        P(head),
        P(head, seq, None),
        P(head, seq, None),
        P(head, seq, None),
        P(),
    )
    return jax.shard_map(
        body, mesh=fine, in_specs=placed, out_specs=P(None, seq + head, None), check_vma=False
    )
```

```python
import math

import jax
import jax.numpy as jnp
from jax import lax
from jax.experimental import pallas as pl
from jax.experimental.pallas import tpu as pltpu
from jax.sharding import Mesh
from jax.sharding import PartitionSpec as P

DH = 256
DF = 512
PART = 128
NS_STEPS = 5
CHIPS = 32
TOK = 128
REACH = 4
RING = ("y_hi", "z")
F32 = jnp.float32
BF = jnp.bfloat16


def matmul(left, right):
    return lax.dot_general(left, right, (((1,), (0,)), ((), ())), preferred_element_type=F32)


def matmul_nt(left, right):
    return lax.dot_general(left, right, (((1,), (1,)), ((), ())), preferred_element_type=F32)


def matmul_tn(left, right):
    return lax.dot_general(left, right, (((0,), (0,)), ((), ())), preferred_element_type=F32)


def halves(wide):
    high = wide.astype(BF)
    return high, (wide - high.astype(F32)).astype(BF)


def rms_norm(values_in):
    wide = values_in.astype(F32)
    mean_square = jnp.mean(wide * wide, axis=-1, keepdims=True)
    return (wide * lax.rsqrt(mean_square + 1e-06)).astype(BF)


def sigmoid(value):
    return 1.0 / (1.0 + jnp.exp(-value))


def fast_forward(query, gate_fast, up_fast, down_fast):
    query_norm = rms_norm(query)
    gate_query = matmul(query_norm, gate_fast)
    up_query = matmul(query_norm, up_fast)
    hidden = (gate_query * sigmoid(gate_query) * up_query).astype(BF)
    return matmul(hidden, down_fast)


def pack_kernel(
    core_ref, q_in, k_in, v_in, rate_in, gate_in, up_in, down_in, mine_ref, other_ref, *scratch
):
    sources = (q_in, k_in, v_in, rate_in, gate_in, up_in, down_in)
    q_ref, k_ref, v_ref, rate_ref, gate_ref, up_ref, down_ref = scratch[:7]
    semaphores = scratch[7]
    copies = [
        pltpu.make_async_copy(source, target, semaphores.at[index])
        for index, (source, target) in enumerate(zip(sources, scratch[:7]))
    ]
    for copy in copies:
        copy.start()
    for copy in copies:
        copy.wait()

    def fill(target, head):
        columns = slice(head * DH, (head + 1) * DH)
        for index, ref in enumerate((q_ref, k_ref, v_ref)):
            for block in range(2):
                first = (index * 2 + block) * 64
                target[first : first + 64, :] = ref[block, :, columns]
        for index, ref in enumerate((gate_ref, up_ref)):
            wide = ref[head].astype(F32)
            pair = jnp.concatenate([wide[:, :DH], wide[:, DH:]], 0)
            target[384 + 8 * index : 392 + 8 * index, :] = pair.astype(BF)
        target[400:408, :] = down_ref[head]
        rate = rate_ref[0, head : head + 1, :]
        high = rate.astype(BF).astype(F32)
        middle = (rate - high).astype(BF).astype(F32)
        low = (rate - high) - middle
        terms = jnp.concatenate([high, middle, low, jnp.zeros_like(rate)], 1)
        target[408:416, :] = jnp.broadcast_to(terms, (8, DH)).astype(BF)

    for head in range(2):

        @pl.when(core_ref[0] == head)
        def _():
            fill(mine_ref, head)
            fill(other_ref, 1 - head)


def arrange_kernel(core_ref, mine_ref, arrived_ref, own_ref, context_ref, pool_ref, weight_ref):
    own_ref[core_ref[0]] = mine_ref[...]
    own_ref[1 - core_ref[0]] = arrived_ref[...]
    for source in range(2):
        context_ref[source] = own_ref[source, 128:384, :]
        for index in range(2):
            first = 128 * index + 64 * source
            rows = slice(128 * (index + 1), 128 * (index + 1) + 64)
            pool_ref[first : first + 64, :] = own_ref[source, rows, :]
        pool_ref[256 + 8 * source : 264 + 8 * source, :] = own_ref[source, 408:416, :]
    for row in range(4):
        lanes = slice(row % 2 * PART, (row % 2 + 1) * PART)
        pieces = []
        for index in range(2):
            first = 384 + 8 * index
            both = [own_ref[src, first : first + 8, lanes].astype(F32) for src in range(2)]
            rows = slice(row // 2 * 4, row // 2 * 4 + 4)
            pieces += [one[rows] for one in both]
        piece = jnp.concatenate(pieces, 0).astype(BF)
        down = jnp.concatenate([own_ref[src, 400:408, :].astype(F32) for src in range(2)], 0)
        down = down.astype(BF)
        for depth in range(8):
            weight_ref[row * 8 + depth, 0:16, :] = piece
            weight_ref[row * 8 + depth, 16:32, :] = down[:, :128]
            weight_ref[row * 8 + depth, 32:48, :] = down[:, 128:]


def grad_kernel(row_ref, p0_ref, p1_ref, p2_ref, p3_ref, raw_ref, grad_ref, slice_ref, down_ref):
    pools = (p0_ref, p1_ref, p2_ref, p3_ref)
    weights = []
    for index in range(2):
        piece = raw_ref[:, 8 * index : 8 * index + 8, :].astype(F32)
        weights.append(piece.reshape(DH, PART).astype(BF))
        slice_ref[index * DH : (index + 1) * DH, :] = weights[index]
        half = raw_ref[:, 16 + 16 * index : 32 + 16 * index, :]
        down_ref[:, index * 128 : (index + 1) * 128] = half.reshape(DF, 128)
    gate_part, up_part = weights
    down_part = down_ref[pl.ds(pl.multiple_of(row_ref[0] * PART, PART), PART), :]
    equal = lax.broadcasted_iota(jnp.int32, (64, 64), 0) == lax.broadcasted_iota(
        jnp.int32, (64, 64), 1
    )
    columns = []
    for pool in pools:
        for source in range(2):
            terms = pool[256 + 8 * source : 264 + 8 * source, :].astype(F32)[0:1]
            rate = terms[:, 0:64] + (terms[:, 64:128] + terms[:, 128:192])
            spread = jnp.where(equal, jnp.broadcast_to(rate, (64, 64)), 0.0)
            columns.append(jnp.sum(spread, axis=1, keepdims=True))
    rate_col = jnp.concatenate(columns, 0)
    keys_now = rms_norm(jnp.concatenate([pool[0:128, :] for pool in pools], 0))
    vals_now = jnp.concatenate([pool[128:256, :] for pool in pools], 0)
    gate_pre = matmul(keys_now, gate_part)
    up_pre = matmul(keys_now, up_part)
    back = matmul_nt(vals_now, down_part)
    sigmoid_val = sigmoid(gate_pre)
    act_val = gate_pre * sigmoid_val
    rate_back = rate_col * back
    d_gate = (rate_back * up_pre * sigmoid_val * (1.0 + gate_pre * (1.0 - sigmoid_val))).astype(BF)
    d_up = (rate_back * act_val).astype(BF)
    h_rate = (rate_col * act_val * up_pre).astype(BF)
    for index, (left, right) in enumerate(
        ((keys_now, d_gate), (keys_now, d_up), (vals_now, h_rate))
    ):
        grad = matmul_tn(left, right).reshape(8, 32, PART)
        grad_ref[:, index * 32 : index * 32 + 32, :] = grad.astype(BF)


def sum_kernel(parts_ref, _, total_ref):
    total = jnp.sum(parts_ref[...].astype(F32), axis=0, keepdims=True)
    total_ref[...] = jnp.broadcast_to(total, (8, 96, PART)).astype(BF)


def widen_kernel(row_ref, piece_ref, f0_ref, f1_ref, f2_ref, f3_ref, _, total_ref, slices_ref):
    for row in range(4):
        total_ref[row] = piece_ref[...]
    for distance, ref in enumerate((f0_ref, f1_ref, f2_ref, f3_ref)):
        slices_ref[lax.rem(row_ref[0] + 4 - distance, 4)] = ref[...]


def whole_weights(slices_ref, index):
    rows = slice(index * DH, (index + 1) * DH)
    return jnp.concatenate([slices_ref[row, rows, :] for row in range(4)], 1)


def attention_kernel(
    chip_ref, own_ref, c1_ref, c2_ref, c3_ref, c4_ref, slices_ref, down_ref, fast_ref, out_ref
):
    chip = chip_ref[0]
    row = lax.broadcasted_iota(jnp.int32, (TOK, TOK), 0)
    column = lax.broadcasted_iota(jnp.int32, (TOK, TOK), 1)
    scale = 1.0 / math.sqrt(DH)
    chunks = (c1_ref, c2_ref, c3_ref, c4_ref)

    def rows_of(distance, index, block):
        if distance == 0:
            first = (2 + 2 * index + block) * 64
            return jnp.concatenate([own_ref[src, first : first + 64, :] for src in range(2)], 0)
        behind = (chip < distance).astype(jnp.int32)
        place = 2 * index + jnp.maximum(block - behind, 0)
        chunk = chunks[distance - 1]
        return jnp.concatenate([chunk[0, place], chunk[1, place]], 0)

    for block in range(2):
        rows = slice(block * 64, block * 64 + 64)
        query = jnp.concatenate([own_ref[0, rows, :], own_ref[1, rows, :]], 0)
        scores = []
        for distance in range(REACH + 1):
            score = matmul_nt(query, rows_of(distance, 0, block)) * scale
            if distance == 0:
                score = jnp.where(row >= column, score, -1e30)
            elif distance == REACH:
                score = jnp.where(row < column, score, -1e30)
            if block == 0 and distance > 0:
                behind = (chip < distance).astype(jnp.int32)
                score = jnp.where(behind + jnp.zeros_like(row) > 0, -1e30, score)
            scores.append(score)
        top = scores[0]
        for score in scores[1:]:
            top = jnp.maximum(top, score)
        row_top = jnp.max(top, axis=-1, keepdims=True)
        exps = [jnp.exp(score - row_top) for score in scores]
        total = exps[0]
        for exp_score in exps[1:]:
            total = total + exp_score
        row_sum = jnp.sum(total, axis=-1, keepdims=True)
        result = None
        for distance in range(REACH + 1):
            weights = (exps[distance] / row_sum).astype(BF)
            part = matmul(weights, rows_of(distance, 1, block))
            result = part if result is None else result + part
        if block == 0:
            gate_fast, up_fast = whole_weights(slices_ref, 0), whole_weights(slices_ref, 1)
            result = result + fast_forward(query, gate_fast, up_fast, down_ref[...])
        else:
            result = result + fast_ref[...]
        out_ref[:, block] = result.reshape(16, 8, DH).astype(BF)


def newton_kernel(step_ref, total_ref, slices_ref, down_ref, own_ref, _, fast_ref, iterate_ref):
    for index in range(3):
        rows = slice(index * 32, index * 32 + 32)
        pieces = [total_ref[row, :, rows, :].astype(F32).reshape(DH, PART) for row in range(4)]
        grad = jnp.concatenate(pieces, 1)
        square = jnp.sum(jnp.sum(grad * grad, axis=0, keepdims=True), axis=1, keepdims=True)
        iterate_ref[index] = grad / (jnp.sqrt(square) + 1e-07)

    def coarse_step(_, carry):
        for index in range(3):
            iterate = iterate_ref[index]
            high = iterate.astype(BF)
            gram = matmul_nt(high, high)
            gram_high = gram.astype(BF)
            poly = -4.775 * gram + 2.0315 * matmul(gram_high, gram_high)
            iterate_ref[index] = 3.4445 * iterate + matmul(poly.astype(BF), high)
        return carry

    def fine_step(_, carry):
        for index in range(3):
            iterate = iterate_ref[index]
            high, low = halves(iterate)
            left = jnp.concatenate([high, high, low], 1)
            gram = matmul_nt(left, jnp.concatenate([high, low, high], 1))
            gram_high, gram_low = halves(gram)
            left = jnp.concatenate([gram_high, gram_high, gram_low], 1)
            square = matmul(left, jnp.concatenate([gram_high, gram_low, gram_high], 0))
            poly_high, poly_low = halves(-4.775 * gram + 2.0315 * square)
            left = jnp.concatenate([poly_high, poly_high, poly_low], 1)
            change = matmul(left, jnp.concatenate([high, low, high], 0))
            iterate_ref[index] = 3.4445 * iterate + change
        return carry

    lax.fori_loop(0, 2, coarse_step, 0)
    lax.fori_loop(0, NS_STEPS - 2, fine_step, 0)
    step = step_ref[0]
    gate_fast = (whole_weights(slices_ref, 0).astype(F32) + step * iterate_ref[0]).astype(BF)
    up_fast = (whole_weights(slices_ref, 1).astype(F32) + step * iterate_ref[1]).astype(BF)
    down_fast = (down_ref[...].astype(F32) + step * iterate_ref[2].T).astype(BF)
    query = jnp.concatenate([own_ref[0, 64:128, :], own_ref[1, 64:128, :]], 0)
    fast_ref[...] = fast_forward(query, gate_fast, up_fast, down_fast)


def norm_kernel(parts_ref, gain_ref, out_ref):
    square = None
    for source in range(16):
        wide = parts_ref[source].astype(F32)
        part = jnp.sum(wide * wide, axis=-1, keepdims=True)
        square = part if square is None else square + part
    scale = lax.rsqrt(square * (1.0 / (16 * DH)) + 1e-06)
    for source in range(16):
        head = 2 * (source % 8) + source // 8
        columns = slice(head * DH, (head + 1) * DH)
        wide = parts_ref[source].astype(F32) * scale * gain_ref[:, columns][None]
        out_ref[:, :, columns] = wide.astype(BF)


PARAMS = pltpu.CompilerParams(vmem_limit_bytes=16 * 1024 * 1024)
VMEM = pl.BlockSpec(memory_space=pltpu.VMEM)
ANY = pl.BlockSpec(memory_space=pl.ANY)
HBM = pl.BlockSpec(memory_space=pltpu.HBM)
SMEM = pl.BlockSpec(memory_space=pltpu.SMEM)


def shape_of(shape, dtype=BF):
    return jax.ShapeDtypeStruct(shape, dtype)


def body(queries, keys, values, token_rates, step_size, w_gate, w_up, w_down, norm_gain):
    core = lax.axis_index("core")
    chip = lax.axis_index(RING).astype(jnp.int32).reshape(1)
    line = lax.axis_index("y_hi").astype(jnp.int32).reshape(1)
    pieces = (queries, keys, values, token_rates, w_gate, w_up, w_down)
    place = core.astype(jnp.int32).reshape(1)
    mine, other = pl.pallas_call(
        pack_kernel,
        out_shape=(shape_of((416, DH)),) * 2,
        in_specs=[SMEM] + [HBM] * 7,
        out_specs=(VMEM,) * 2,
        scratch_shapes=[pltpu.VMEM(piece.shape, piece.dtype) for piece in pieces]
        + [pltpu.SemaphoreType.DMA((7,))],
        compiler_params=pltpu.CompilerParams(vmem_limit_bytes=61500 * 1024),
        name="pack",
    )(place, *pieces)
    arrived = lax.ppermute(other, "core", [(0, 1), (1, 0)])
    own, context, pool, raw = pl.pallas_call(
        arrange_kernel,
        out_shape=(
            shape_of((2, 416, DH)),
            shape_of((2, 256, DH)),
            shape_of((272, DH)),
            shape_of((CHIPS, 48, 128)),
        ),
        in_specs=[SMEM, VMEM, VMEM],
        out_specs=(VMEM,) * 4,
        compiler_params=PARAMS,
        name="arrange",
    )(place, mine, arrived)
    raw = lax.all_to_all(raw, RING, 0, 0, tiled=True)
    pools = [pool]
    for distance in range(1, 4):
        pools.append(lax.ppermute(pool, "y_hi", [(i, (i + distance) % 4) for i in range(4)]))
    ring = [(i, (i + 1) % CHIPS) for i in range(CHIPS)]
    chunks = [lax.ppermute(context, RING, ring)]

    grad, slices, down_fast = pl.pallas_call(
        grad_kernel,
        out_shape=(shape_of((8, 96, PART)), shape_of((2 * DH, PART)), shape_of((DF, DH))),
        in_specs=[SMEM] + [VMEM] * 5,
        out_specs=(VMEM,) * 3,
        compiler_params=PARAMS,
        name="grad",
    )(line, *pools, raw)
    parts = lax.all_to_all(grad, "z", 0, 0, tiled=True)
    fills = [slices]
    for distance in range(1, 4):
        fills.append(lax.ppermute(slices, "y_hi", [(i, (i + distance) % 4) for i in range(4)]))
    total = pl.pallas_call(
        sum_kernel,
        out_shape=shape_of((8, 96, PART)),
        in_specs=[VMEM, ANY],
        out_specs=VMEM,
        compiler_params=PARAMS,
        name="sum",
    )(parts, chunks[0])
    chunks.append(lax.ppermute(chunks[-1], RING, ring))
    total = lax.all_to_all(total, "z", 0, 0, tiled=True)
    total, slices = pl.pallas_call(
        widen_kernel,
        out_shape=(shape_of((4, 8, 96, PART)), shape_of((4, 2 * DH, PART))),
        in_specs=[SMEM] + [VMEM] * 5 + [ANY],
        out_specs=(VMEM,) * 2,
        compiler_params=PARAMS,
        name="widen",
    )(line, total, *fills, chunks[1])
    chunks.append(lax.ppermute(chunks[-1], RING, ring))
    total = lax.all_to_all(total, "y_hi", 0, 0, tiled=True)

    step = lax.dynamic_slice_in_dim(step_size, core, 1, 0)
    fast = pl.pallas_call(
        newton_kernel,
        out_shape=shape_of((TOK, DH), F32),
        in_specs=[SMEM] + [VMEM] * 4 + [ANY],
        out_specs=VMEM,
        scratch_shapes=[pltpu.VMEM((3, DH, DF), F32)],
        compiler_params=PARAMS,
        cost_estimate=pl.CostEstimate(
            flops=8_000_000_000, transcendentals=100_000, bytes_accessed=4_000_000
        ),
        name="newton",
    )(step, total, slices, down_fast, own, chunks[2])
    chunks.append(lax.ppermute(chunks[-1], RING, ring))
    chunks = [chunk.reshape(2, 4, 64, DH) for chunk in chunks]
    combined = pl.pallas_call(
        attention_kernel,
        out_shape=shape_of((16, 2, 8, DH)),
        in_specs=[SMEM] + [VMEM] * 8,
        out_specs=VMEM,
        compiler_params=PARAMS,
        name="window",
    )(chip, own, *chunks, slices, down_fast, fast)
    gathered = lax.all_to_all(combined, ("core", "y_lo", "x"), 0, 0, tiled=True)
    return pl.pallas_call(
        norm_kernel,
        out_shape=jax.ShapeDtypeStruct((2, 8, 16 * DH), BF),
        in_specs=[VMEM] * 2,
        out_specs=VMEM,
        compiler_params=PARAMS,
        name="norm",
    )(gathered, norm_gain.reshape(1, 16 * DH))


def solution(mesh):
    fine = Mesh(mesh.devices.reshape(2, 4, 4, 8, 2), ("y_lo", "x", "y_hi", "z", "core"))
    seq = RING + ("core",)
    head = ("y_lo", "x")
    placed = (
        P(None, seq, head),
        P(None, seq, head),
        P(None, seq, head),
        P(None, head, seq),
        P(head),
        P(head, seq, None),
        P(head, seq, None),
        P(head, seq, None),
        P(),
    )
    return jax.shard_map(
        body, mesh=fine, in_specs=placed, out_specs=P(None, seq + head, None), check_vma=False
    )
```

```python
import math

import jax
import jax.numpy as jnp
from jax import lax
from jax.experimental import pallas as pl
from jax.experimental.pallas import tpu as pltpu
from jax.sharding import Mesh
from jax.sharding import PartitionSpec as P

DH = 256
DF = 512
PART = 128
NS_STEPS = 5
CHIPS = 32
TOK = 128
REACH = 4
RING = ("y_hi", "z")
F32 = jnp.float32
BF = jnp.bfloat16


def matmul(left, right):
    return lax.dot_general(left, right, (((1,), (0,)), ((), ())), preferred_element_type=F32)


def matmul_nt(left, right):
    return lax.dot_general(left, right, (((1,), (1,)), ((), ())), preferred_element_type=F32)


def matmul_tn(left, right):
    return lax.dot_general(left, right, (((0,), (0,)), ((), ())), preferred_element_type=F32)


def halves(wide):
    high = wide.astype(BF)
    return high, (wide - high.astype(F32)).astype(BF)


def rms_norm(values_in):
    wide = values_in.astype(F32)
    mean_square = jnp.mean(wide * wide, axis=-1, keepdims=True)
    return (wide * lax.rsqrt(mean_square + 1e-06)).astype(BF)


def sigmoid(value):
    return 1.0 / (1.0 + jnp.exp(-value))


def fast_forward(query, gate_fast, up_fast, down_fast):
    query_norm = rms_norm(query)
    gate_query = matmul(query_norm, gate_fast)
    up_query = matmul(query_norm, up_fast)
    hidden = (gate_query * sigmoid(gate_query) * up_query).astype(BF)
    return matmul(hidden, down_fast)


def pack_kernel(
    core_ref, q_in, k_in, v_in, rate_in, gate_in, up_in, down_in, mine_ref, other_ref, deal_ref, *scratch
):
    sources = (q_in, k_in, v_in, rate_in, gate_in, up_in, down_in)
    q_ref, k_ref, v_ref, rate_ref, gate_ref, up_ref, down_ref = scratch[:7]
    semaphores = scratch[7]
    copies = [
        pltpu.make_async_copy(source, target, semaphores.at[index])
        for index, (source, target) in enumerate(zip(sources, scratch[:7]))
    ]
    for copy in copies:
        copy.start()
    for copy in copies:
        copy.wait()

    def fill(target, head):
        columns = slice(head * DH, (head + 1) * DH)
        for index, ref in enumerate((q_ref, k_ref, v_ref)):
            for block in range(2):
                first = (index * 2 + block) * 64
                target[first : first + 64, :] = ref[block, :, columns]
        rate = rate_ref[0, head : head + 1, :]
        high = rate.astype(BF).astype(F32)
        middle = (rate - high).astype(BF).astype(F32)
        low = (rate - high) - middle
        terms = jnp.concatenate([high, middle, low, jnp.zeros_like(rate)], 1)
        target[384:392, :] = jnp.broadcast_to(terms, (8, DH)).astype(BF)

    for head in range(2):

        @pl.when(core_ref[0] == head)
        def _():
            fill(mine_ref, head)
            fill(other_ref, 1 - head)

        tiles = []
        for row in range(4):
            part = slice(row * PART, (row + 1) * PART)
            pair = [gate_ref[head, :, part].astype(F32), up_ref[head, :, part].astype(F32)]
            tiles.append(jnp.concatenate(pair, 0))
        tiles += [down_ref[head, :, :128].astype(F32), down_ref[head, :, 128:].astype(F32)]
        piece = jnp.concatenate(tiles, 0).astype(BF)
        for depth in range(8):
            deal_ref[2 * depth + head] = piece


def arrange_kernel(core_ref, mine_ref, arrived_ref, own_ref, context_ref):
    own_ref[core_ref[0]] = mine_ref[...]
    own_ref[1 - core_ref[0]] = arrived_ref[...]
    for source in range(2):
        context_ref[source] = own_ref[source, 128:384, :]


def merge_kernel(own_ref, dealt_ref, pool_ref, down_ref):
    out_row = lax.broadcasted_iota(jnp.int32, (128, 128), 0)
    in_row = lax.broadcasted_iota(jnp.int32, (128, 128), 1)
    place = out_row % 64
    pick = (place // 4) * 8 + (out_row // 64) * 4 + place % 4
    chosen = jnp.where(in_row == pick, 1.0, 0.0).astype(BF)
    for row in range(4):
        for source in range(2):
            for index in range(2):
                first = 128 * index + 64 * source
                rows = slice(128 * (index + 1), 128 * (index + 1) + 64)
                pool_ref[row, first : first + 64, :] = own_ref[source, rows, :]
            first = 256 + 8 * source
            pool_ref[row, first : first + 8, :] = own_ref[source, 384:392, :]
        mixed = dealt_ref[:, 8 * row : 8 * row + 8, :].astype(F32).reshape(128, PART).astype(BF)
        ordered = matmul(chosen, mixed).astype(BF)
        pool_ref[row, 272:336, :128] = ordered[:64]
        pool_ref[row, 272:336, 128:] = ordered[64:]
    for index in range(2):
        half = dealt_ref[:, 32 + 8 * index : 40 + 8 * index, :].astype(F32)
        down_ref[:, index * 128 : (index + 1) * 128] = half.reshape(PART, 128).astype(BF)


def grad_kernel(pool_ref, down_ref, grad_ref, slice_ref):
    slice_ref[0:DH, :] = pool_ref[:, 272:336, :].reshape(DH, DH)
    slice_ref[DH:, :] = down_ref[...]
    weights = (slice_ref[0:DH, :PART], slice_ref[0:DH, PART:])
    gate_part, up_part = weights
    down_part = down_ref[...]
    equal = lax.broadcasted_iota(jnp.int32, (64, 64), 0) == lax.broadcasted_iota(
        jnp.int32, (64, 64), 1
    )
    columns = []
    for row in range(4):
        for source in range(2):
            terms = pool_ref[row, 256 + 8 * source : 264 + 8 * source, :].astype(F32)[0:1]
            rate = terms[:, 0:64] + (terms[:, 64:128] + terms[:, 128:192])
            spread = jnp.where(equal, jnp.broadcast_to(rate, (64, 64)), 0.0)
            columns.append(jnp.sum(spread, axis=1, keepdims=True))
    rate_col = jnp.concatenate(columns, 0)
    keys_now = rms_norm(pool_ref[:, 0:128, :].reshape(4 * TOK, DH))
    vals_now = pool_ref[:, 128:256, :].reshape(4 * TOK, DH)
    gate_pre = matmul(keys_now, gate_part)
    up_pre = matmul(keys_now, up_part)
    back = matmul_nt(vals_now, down_part)
    sigmoid_val = sigmoid(gate_pre)
    act_val = gate_pre * sigmoid_val
    rate_back = rate_col * back
    d_gate = (rate_back * up_pre * sigmoid_val * (1.0 + gate_pre * (1.0 - sigmoid_val))).astype(BF)
    d_up = (rate_back * act_val).astype(BF)
    h_rate = (rate_col * act_val * up_pre).astype(BF)
    for index, (left, right) in enumerate(
        ((keys_now, d_gate), (keys_now, d_up), (vals_now, h_rate))
    ):
        grad = matmul_tn(left, right).reshape(8, 32, PART)
        grad_ref[:, index * 32 : index * 32 + 32, :] = grad.astype(BF)


def sum_kernel(parts_ref, total_ref):
    total = jnp.sum(parts_ref[...].astype(F32), axis=0, keepdims=True)
    total_ref[...] = jnp.broadcast_to(total, (8, 96, PART)).astype(BF)


def widen_kernel(piece_ref, total_ref):
    for row in range(4):
        total_ref[row] = piece_ref[...]


def whole_weights(slices_ref):
    gate_fast = jnp.concatenate([slices_ref[row, 0:DH, :PART] for row in range(4)], 1)
    up_fast = jnp.concatenate([slices_ref[row, 0:DH, PART:] for row in range(4)], 1)
    return gate_fast, up_fast, slices_ref[:, DH:, :].reshape(DF, DH)


def attention_kernel(
    chip_ref, own_ref, c1_ref, c2_ref, c3_ref, c4_ref, slices_ref, fast_ref, out_ref
):
    chip = chip_ref[0]
    row = lax.broadcasted_iota(jnp.int32, (TOK, TOK), 0)
    column = lax.broadcasted_iota(jnp.int32, (TOK, TOK), 1)
    scale = 1.0 / math.sqrt(DH)
    chunks = (c1_ref, c2_ref, c3_ref, c4_ref)

    def rows_of(distance, index, block):
        if distance == 0:
            first = (2 + 2 * index + block) * 64
            return jnp.concatenate([own_ref[src, first : first + 64, :] for src in range(2)], 0)
        behind = (chip < distance).astype(jnp.int32)
        place = 2 * index + jnp.maximum(block - behind, 0)
        chunk = chunks[distance - 1]
        return jnp.concatenate([chunk[0, place], chunk[1, place]], 0)

    for block in range(2):
        rows = slice(block * 64, block * 64 + 64)
        query = jnp.concatenate([own_ref[0, rows, :], own_ref[1, rows, :]], 0)
        scores = []
        for distance in range(REACH + 1):
            score = matmul_nt(query, rows_of(distance, 0, block)) * scale
            if distance == 0:
                score = jnp.where(row >= column, score, -1e30)
            elif distance == REACH:
                score = jnp.where(row < column, score, -1e30)
            if block == 0 and distance > 0:
                behind = (chip < distance).astype(jnp.int32)
                score = jnp.where(behind + jnp.zeros_like(row) > 0, -1e30, score)
            scores.append(score)
        top = scores[0]
        for score in scores[1:]:
            top = jnp.maximum(top, score)
        row_top = jnp.max(top, axis=-1, keepdims=True)
        exps = [jnp.exp(score - row_top) for score in scores]
        total = exps[0]
        for exp_score in exps[1:]:
            total = total + exp_score
        row_sum = jnp.sum(total, axis=-1, keepdims=True)
        result = None
        for distance in range(REACH + 1):
            weights = (exps[distance] / row_sum).astype(BF)
            part = matmul(weights, rows_of(distance, 1, block))
            result = part if result is None else result + part
        if block == 0:
            result = result + fast_forward(query, *whole_weights(slices_ref))
        else:
            result = result + fast_ref[...]
        out_ref[:, block] = result.reshape(16, 8, DH).astype(BF)


def newton_kernel(
    step_ref,
    row_ref,
    total_ref,
    f0_ref,
    f1_ref,
    f2_ref,
    f3_ref,
    own_ref,
    _,
    fast_ref,
    slices_ref,
    iterate_ref,
):
    for distance, ref in enumerate((f0_ref, f1_ref, f2_ref, f3_ref)):
        slices_ref[lax.rem(row_ref[0] + 4 - distance, 4)] = ref[...]
    for index in range(3):
        rows = slice(index * 32, index * 32 + 32)
        pieces = [total_ref[row, :, rows, :].astype(F32).reshape(DH, PART) for row in range(4)]
        grad = jnp.concatenate(pieces, 1)
        square = jnp.sum(jnp.sum(grad * grad, axis=0, keepdims=True), axis=1, keepdims=True)
        iterate_ref[index] = grad / (jnp.sqrt(square) + 1e-07)

    def coarse_step(_, carry):
        for index in range(3):
            iterate = iterate_ref[index]
            high = iterate.astype(BF)
            gram = matmul_nt(high, high)
            gram_high = gram.astype(BF)
            poly = -4.775 * gram + 2.0315 * matmul(gram_high, gram_high)
            iterate_ref[index] = 3.4445 * iterate + matmul(poly.astype(BF), high)
        return carry

    def fine_step(_, carry):
        for index in range(3):
            iterate = iterate_ref[index]
            high, low = halves(iterate)
            left = jnp.concatenate([high, high, low], 1)
            gram = matmul_nt(left, jnp.concatenate([high, low, high], 1))
            gram_high, gram_low = halves(gram)
            left = jnp.concatenate([gram_high, gram_high, gram_low], 1)
            square = matmul(left, jnp.concatenate([gram_high, gram_low, gram_high], 0))
            poly_high, poly_low = halves(-4.775 * gram + 2.0315 * square)
            left = jnp.concatenate([poly_high, poly_high, poly_low], 1)
            change = matmul(left, jnp.concatenate([high, low, high], 0))
            iterate_ref[index] = 3.4445 * iterate + change
        return carry

    lax.fori_loop(0, 2, coarse_step, 0)
    lax.fori_loop(0, NS_STEPS - 2, fine_step, 0)
    step = step_ref[0]
    gate_fast, up_fast, down_fast = whole_weights(slices_ref)
    gate_fast = (gate_fast.astype(F32) + step * iterate_ref[0]).astype(BF)
    up_fast = (up_fast.astype(F32) + step * iterate_ref[1]).astype(BF)
    down_fast = (down_fast.astype(F32) + step * iterate_ref[2].T).astype(BF)
    query = jnp.concatenate([own_ref[0, 64:128, :], own_ref[1, 64:128, :]], 0)
    fast_ref[...] = fast_forward(query, gate_fast, up_fast, down_fast)


def norm_kernel(parts_ref, gain_ref, out_ref):
    square = None
    for source in range(16):
        wide = parts_ref[source].astype(F32)
        part = jnp.sum(wide * wide, axis=-1, keepdims=True)
        square = part if square is None else square + part
    scale = lax.rsqrt(square * (1.0 / (16 * DH)) + 1e-06)
    for source in range(16):
        head = 2 * (source % 8) + source // 8
        columns = slice(head * DH, (head + 1) * DH)
        wide = parts_ref[source].astype(F32) * scale * gain_ref[:, columns][None]
        out_ref[:, :, columns] = wide.astype(BF)


PARAMS = pltpu.CompilerParams(vmem_limit_bytes=16 * 1024 * 1024)
VMEM = pl.BlockSpec(memory_space=pltpu.VMEM)
ANY = pl.BlockSpec(memory_space=pl.ANY)
HBM = pl.BlockSpec(memory_space=pltpu.HBM)
SMEM = pl.BlockSpec(memory_space=pltpu.SMEM)


def shape_of(shape, dtype=BF):
    return jax.ShapeDtypeStruct(shape, dtype)


def body(queries, keys, values, token_rates, step_size, w_gate, w_up, w_down, norm_gain):
    core = lax.axis_index("core")
    chip = lax.axis_index(RING).astype(jnp.int32).reshape(1)
    line = lax.axis_index("y_hi").astype(jnp.int32).reshape(1)
    pieces = (queries, keys, values, token_rates, w_gate, w_up, w_down)
    place = core.astype(jnp.int32).reshape(1)
    mine, other, dealt = pl.pallas_call(
        pack_kernel,
        out_shape=(shape_of((392, DH)), shape_of((392, DH)), shape_of((16, 48, 128))),
        in_specs=[SMEM] + [HBM] * 7,
        out_specs=(VMEM,) * 3,
        scratch_shapes=[pltpu.VMEM(piece.shape, piece.dtype) for piece in pieces]
        + [pltpu.SemaphoreType.DMA((7,))],
        compiler_params=pltpu.CompilerParams(vmem_limit_bytes=61500 * 1024),
        name="pack",
    )(place, *pieces)
    dealt = lax.all_to_all(dealt, ("z", "core"), 0, 0, tiled=True)
    arrived = lax.ppermute(other, "core", [(0, 1), (1, 0)])
    own, context = pl.pallas_call(
        arrange_kernel,
        out_shape=(shape_of((2, 392, DH)), shape_of((2, 256, DH))),
        in_specs=[SMEM, VMEM, VMEM],
        out_specs=(VMEM,) * 2,
        compiler_params=PARAMS,
        name="arrange",
    )(place, mine, arrived)
    ring = [(i, (i + 1) % CHIPS) for i in range(CHIPS)]
    chunks = [lax.ppermute(context, RING, ring)]
    pool, down = pl.pallas_call(
        merge_kernel,
        out_shape=(shape_of((4, 336, DH)), shape_of((PART, DH))),
        in_specs=[VMEM] * 2,
        out_specs=(VMEM,) * 2,
        compiler_params=PARAMS,
        name="merge",
    )(own, dealt)
    pool = lax.all_to_all(pool, "y_hi", 0, 0, tiled=True)

    grad, slices = pl.pallas_call(
        grad_kernel,
        out_shape=(shape_of((8, 96, PART)), shape_of((384, DH))),
        in_specs=[VMEM] * 2,
        out_specs=(VMEM,) * 2,
        compiler_params=PARAMS,
        name="grad",
    )(pool, down)
    parts = lax.all_to_all(grad, "z", 0, 0, tiled=True)
    fills = [slices]
    for distance in range(1, 4):
        fills.append(lax.ppermute(slices, "y_hi", [(i, (i + distance) % 4) for i in range(4)]))
    chunks.append(lax.ppermute(chunks[-1], RING, ring))
    total = pl.pallas_call(
        sum_kernel,
        out_shape=shape_of((8, 96, PART)),
        in_specs=[VMEM],
        out_specs=VMEM,
        compiler_params=PARAMS,
        name="sum",
    )(parts)
    total = lax.all_to_all(total, "z", 0, 0, tiled=True)
    chunks.append(lax.ppermute(chunks[-1], RING, ring))
    total = pl.pallas_call(
        widen_kernel,
        out_shape=shape_of((4, 8, 96, PART)),
        in_specs=[VMEM],
        out_specs=VMEM,
        compiler_params=PARAMS,
        name="widen",
    )(total)
    total = lax.all_to_all(total, "y_hi", 0, 0, tiled=True)

    step = lax.dynamic_slice_in_dim(step_size, core, 1, 0)
    fast, slices = pl.pallas_call(
        newton_kernel,
        out_shape=(shape_of((TOK, DH), F32), shape_of((4, 384, DH))),
        in_specs=[SMEM] * 2 + [VMEM] * 6 + [ANY],
        out_specs=(VMEM,) * 2,
        scratch_shapes=[pltpu.VMEM((3, DH, DF), F32)],
        compiler_params=PARAMS,
        cost_estimate=pl.CostEstimate(
            flops=8_000_000_000, transcendentals=100_000, bytes_accessed=4_000_000
        ),
        name="newton",
    )(step, line, total, *fills, own, chunks[2])
    chunks.append(lax.ppermute(chunks[-1], RING, ring))
    chunks = [chunk.reshape(2, 4, 64, DH) for chunk in chunks]
    combined = pl.pallas_call(
        attention_kernel,
        out_shape=shape_of((16, 2, 8, DH)),
        in_specs=[SMEM] + [VMEM] * 7,
        out_specs=VMEM,
        compiler_params=PARAMS,
        name="window",
    )(chip, own, *chunks, slices, fast)
    gathered = lax.all_to_all(combined, ("core", "y_lo", "x"), 0, 0, tiled=True)
    return pl.pallas_call(
        norm_kernel,
        out_shape=jax.ShapeDtypeStruct((2, 8, 16 * DH), BF),
        in_specs=[VMEM] * 2,
        out_specs=VMEM,
        compiler_params=PARAMS,
        name="norm",
    )(gathered, norm_gain.reshape(1, 16 * DH))


def solution(mesh):
    fine = Mesh(mesh.devices.reshape(2, 4, 4, 8, 2), ("y_lo", "x", "y_hi", "z", "core"))
    seq = RING + ("core",)
    head = ("y_lo", "x")
    placed = (
        P(None, seq, head),
        P(None, seq, head),
        P(None, seq, head),
        P(None, head, seq),
        P(head),
        P(head, seq, None),
        P(head, seq, None),
        P(head, seq, None),
        P(),
    )
    return jax.shard_map(
        body, mesh=fine, in_specs=placed, out_specs=P(None, seq + head, None), check_vma=False
    )
```

```python
import math

import jax
import jax.numpy as jnp
from jax import lax
from jax.experimental import pallas as pl
from jax.experimental.pallas import tpu as pltpu
from jax.sharding import Mesh
from jax.sharding import PartitionSpec as P

DH = 256
DF = 512
PART = 128
NS_STEPS = 5
CHIPS = 32
TOK = 128
REACH = 4
RING = ("y_hi", "z")
F32 = jnp.float32
BF = jnp.bfloat16


def matmul(left, right):
    return lax.dot_general(left, right, (((1,), (0,)), ((), ())), preferred_element_type=F32)


def matmul_nt(left, right):
    return lax.dot_general(left, right, (((1,), (1,)), ((), ())), preferred_element_type=F32)


def matmul_tn(left, right):
    return lax.dot_general(left, right, (((0,), (0,)), ((), ())), preferred_element_type=F32)


def halves(wide):
    high = wide.astype(BF)
    return high, (wide - high.astype(F32)).astype(BF)


def rms_norm(values_in):
    wide = values_in.astype(F32)
    mean_square = jnp.mean(wide * wide, axis=-1, keepdims=True)
    return (wide * lax.rsqrt(mean_square + 1e-06)).astype(BF)


def sigmoid(value):
    return 1.0 / (1.0 + jnp.exp(-value))


def fast_forward(query, gate_fast, up_fast, down_fast):
    query_norm = rms_norm(query)
    gate_query = matmul(query_norm, gate_fast)
    up_query = matmul(query_norm, up_fast)
    hidden = (gate_query * sigmoid(gate_query) * up_query).astype(BF)
    return matmul(hidden, down_fast)


def pack_kernel(
    core_ref, q_in, k_in, v_in, rate_in, gate_in, up_in, down_in, mine_ref, other_ref, deal_ref, *scratch
):
    sources = (q_in, k_in, v_in, rate_in, gate_in, up_in, down_in)
    q_ref, k_ref, v_ref, rate_ref, gate_ref, up_ref, down_ref = scratch[:7]
    semaphores = scratch[7]
    copies = [
        pltpu.make_async_copy(source, target, semaphores.at[index])
        for index, (source, target) in enumerate(zip(sources, scratch[:7]))
    ]
    for copy in copies:
        copy.start()
    for copy in copies:
        copy.wait()

    def fill(target, head):
        columns = slice(head * DH, (head + 1) * DH)
        for index, ref in enumerate((q_ref, k_ref, v_ref)):
            for block in range(2):
                first = (index * 2 + block) * 64
                target[first : first + 64, :] = ref[block, :, columns]
        rate = rate_ref[0, head : head + 1, :]
        high = rate.astype(BF).astype(F32)
        middle = (rate - high).astype(BF).astype(F32)
        low = (rate - high) - middle
        terms = jnp.concatenate([high, middle, low, jnp.zeros_like(rate)], 1)
        target[384:392, :] = jnp.broadcast_to(terms, (8, DH)).astype(BF)

    for head in range(2):

        @pl.when(core_ref[0] == head)
        def _():
            fill(mine_ref, head)
            fill(other_ref, 1 - head)

        tiles = []
        for ref in (gate_ref, up_ref):
            wide = ref[head].astype(F32)
            tiles += [wide[:, :DH], wide[:, DH:]]
        tiles.append(down_ref[head].astype(F32))
        piece = jnp.concatenate(tiles, 0).astype(BF)
        for target in range(CHIPS):
            deal_ref[2 * target + head] = piece


def arrange_kernel(core_ref, mine_ref, arrived_ref, own_ref, context_ref, pool_ref):
    own_ref[core_ref[0]] = mine_ref[...]
    own_ref[1 - core_ref[0]] = arrived_ref[...]
    for source in range(2):
        context_ref[source] = own_ref[source, 128:384, :]
        for index in range(2):
            first = 128 * index + 64 * source
            rows = slice(128 * (index + 1), 128 * (index + 1) + 64)
            pool_ref[first : first + 64, :] = own_ref[source, rows, :]
        pool_ref[256 + 8 * source : 264 + 8 * source, :] = own_ref[source, 384:392, :]


def grad_kernel(row_ref, p0_ref, p1_ref, p2_ref, p3_ref, raw_ref, grad_ref, slices_ref, down_ref):
    pools = (p0_ref, p1_ref, p2_ref, p3_ref)
    out_row = lax.broadcasted_iota(jnp.int32, (DH, 2 * DH), 0)
    in_row = lax.broadcasted_iota(jnp.int32, (DH, 2 * DH), 1)
    for index in range(2):
        mixed = raw_ref[:, 8 * index : 8 * index + 8, :].astype(F32)
        mixed = mixed.reshape(2 * DH, DH).astype(BF)
        rows = slice(index * DH, (index + 1) * DH)
        for half in range(2):
            pick = (out_row // 4) * 8 + half * 4 + out_row % 4
            chosen = jnp.where(in_row == pick, 1.0, 0.0).astype(BF)
            ordered = matmul(chosen, mixed).astype(BF)
            slices_ref[2 * half, rows, :] = ordered[:, :PART]
            slices_ref[2 * half + 1, rows, :] = ordered[:, PART:]
    down_ref[...] = raw_ref[:, 16:24, :].astype(F32).reshape(DF, DH).astype(BF)
    row = row_ref[0]
    weights = (slices_ref[row, :DH, :], slices_ref[row, DH:, :])
    down_part = down_ref[pl.ds(pl.multiple_of(row * PART, PART), PART), :]
    equal = lax.broadcasted_iota(jnp.int32, (64, 64), 0) == lax.broadcasted_iota(
        jnp.int32, (64, 64), 1
    )
    columns = []
    for pool in pools:
        for source in range(2):
            terms = pool[256 + 8 * source : 264 + 8 * source, :].astype(F32)[0:1]
            rate = terms[:, 0:64] + (terms[:, 64:128] + terms[:, 128:192])
            spread = jnp.where(equal, jnp.broadcast_to(rate, (64, 64)), 0.0)
            columns.append(jnp.sum(spread, axis=1, keepdims=True))
    rate_col = jnp.concatenate(columns, 0)
    gate_part, up_part = weights
    keys_now = rms_norm(jnp.concatenate([pool[0:128, :] for pool in pools], 0))
    vals_now = jnp.concatenate([pool[128:256, :] for pool in pools], 0)
    gate_pre = matmul(keys_now, gate_part)
    up_pre = matmul(keys_now, up_part)
    back = matmul_nt(vals_now, down_part)
    sigmoid_val = sigmoid(gate_pre)
    act_val = gate_pre * sigmoid_val
    rate_back = rate_col * back
    d_gate = (rate_back * up_pre * sigmoid_val * (1.0 + gate_pre * (1.0 - sigmoid_val))).astype(BF)
    d_up = (rate_back * act_val).astype(BF)
    h_rate = (rate_col * act_val * up_pre).astype(BF)
    for index, (left, right) in enumerate(
        ((keys_now, d_gate), (keys_now, d_up), (vals_now, h_rate))
    ):
        grad = matmul_tn(left, right).reshape(8, 32, PART)
        grad_ref[:, index * 32 : index * 32 + 32, :] = grad.astype(BF)


def sum_kernel(parts_ref, total_ref):
    total = jnp.sum(parts_ref[...].astype(F32), axis=0, keepdims=True)
    total_ref[...] = jnp.broadcast_to(total, (8, 96, PART)).astype(BF)


def widen_kernel(piece_ref, total_ref):
    for row in range(4):
        total_ref[row] = piece_ref[...]


def whole_weights(slices_ref):
    gate_fast = jnp.concatenate([slices_ref[row, :DH, :] for row in range(4)], 1)
    up_fast = jnp.concatenate([slices_ref[row, DH:, :] for row in range(4)], 1)
    return gate_fast, up_fast


def attention_kernel(
    chip_ref, own_ref, c1_ref, c2_ref, c3_ref, c4_ref, slices_ref, down_ref, fast_ref, out_ref
):
    chip = chip_ref[0]
    row = lax.broadcasted_iota(jnp.int32, (TOK, TOK), 0)
    column = lax.broadcasted_iota(jnp.int32, (TOK, TOK), 1)
    scale = 1.0 / math.sqrt(DH)
    chunks = (c1_ref, c2_ref, c3_ref, c4_ref)

    def rows_of(distance, index, block):
        if distance == 0:
            first = (2 + 2 * index + block) * 64
            return jnp.concatenate([own_ref[src, first : first + 64, :] for src in range(2)], 0)
        behind = (chip < distance).astype(jnp.int32)
        place = 2 * index + jnp.maximum(block - behind, 0)
        chunk = chunks[distance - 1]
        return jnp.concatenate([chunk[0, place], chunk[1, place]], 0)

    for block in range(2):
        rows = slice(block * 64, block * 64 + 64)
        query = jnp.concatenate([own_ref[0, rows, :], own_ref[1, rows, :]], 0)
        scores = []
        for distance in range(REACH + 1):
            score = matmul_nt(query, rows_of(distance, 0, block)) * scale
            if distance == 0:
                score = jnp.where(row >= column, score, -1e30)
            elif distance == REACH:
                score = jnp.where(row < column, score, -1e30)
            if block == 0 and distance > 0:
                behind = (chip < distance).astype(jnp.int32)
                score = jnp.where(behind + jnp.zeros_like(row) > 0, -1e30, score)
            scores.append(score)
        top = scores[0]
        for score in scores[1:]:
            top = jnp.maximum(top, score)
        row_top = jnp.max(top, axis=-1, keepdims=True)
        exps = [jnp.exp(score - row_top) for score in scores]
        total = exps[0]
        for exp_score in exps[1:]:
            total = total + exp_score
        row_sum = jnp.sum(total, axis=-1, keepdims=True)
        result = None
        for distance in range(REACH + 1):
            weights = (exps[distance] / row_sum).astype(BF)
            part = matmul(weights, rows_of(distance, 1, block))
            result = part if result is None else result + part
        if block == 0:
            result = result + fast_forward(query, *whole_weights(slices_ref), down_ref[...])
        else:
            result = result + fast_ref[...]
        out_ref[:, block] = result.reshape(16, 8, DH).astype(BF)


def newton_kernel(
    step_ref, total_ref, slices_ref, down_ref, own_ref, _, fast_ref, iterate_ref
):
    for index in range(3):
        rows = slice(index * 32, index * 32 + 32)
        pieces = [total_ref[row, :, rows, :].astype(F32).reshape(DH, PART) for row in range(4)]
        grad = jnp.concatenate(pieces, 1)
        square = jnp.sum(jnp.sum(grad * grad, axis=0, keepdims=True), axis=1, keepdims=True)
        iterate_ref[index] = grad / (jnp.sqrt(square) + 1e-07)

    def coarse_step(_, carry):
        for index in range(3):
            iterate = iterate_ref[index]
            high = iterate.astype(BF)
            gram = matmul_nt(high, high)
            gram_high = gram.astype(BF)
            poly = -4.775 * gram + 2.0315 * matmul(gram_high, gram_high)
            iterate_ref[index] = 3.4445 * iterate + matmul(poly.astype(BF), high)
        return carry

    def fine_step(_, carry):
        for index in range(3):
            iterate = iterate_ref[index]
            high, low = halves(iterate)
            left = jnp.concatenate([high, high, low], 1)
            gram = matmul_nt(left, jnp.concatenate([high, low, high], 1))
            gram_high, gram_low = halves(gram)
            left = jnp.concatenate([gram_high, gram_high, gram_low], 1)
            square = matmul(left, jnp.concatenate([gram_high, gram_low, gram_high], 0))
            poly_high, poly_low = halves(-4.775 * gram + 2.0315 * square)
            left = jnp.concatenate([poly_high, poly_high, poly_low], 1)
            change = matmul(left, jnp.concatenate([high, low, high], 0))
            iterate_ref[index] = 3.4445 * iterate + change
        return carry

    lax.fori_loop(0, 2, coarse_step, 0)
    lax.fori_loop(0, NS_STEPS - 2, fine_step, 0)
    step = step_ref[0]
    gate_fast, up_fast = whole_weights(slices_ref)
    gate_fast = (gate_fast.astype(F32) + step * iterate_ref[0]).astype(BF)
    up_fast = (up_fast.astype(F32) + step * iterate_ref[1]).astype(BF)
    down_fast = (down_ref[...].astype(F32) + step * iterate_ref[2].T).astype(BF)
    query = jnp.concatenate([own_ref[0, 64:128, :], own_ref[1, 64:128, :]], 0)
    fast_ref[...] = fast_forward(query, gate_fast, up_fast, down_fast)


def norm_kernel(parts_ref, gain_ref, out_ref):
    square = None
    for source in range(16):
        wide = parts_ref[source].astype(F32)
        part = jnp.sum(wide * wide, axis=-1, keepdims=True)
        square = part if square is None else square + part
    scale = lax.rsqrt(square * (1.0 / (16 * DH)) + 1e-06)
    for source in range(16):
        head = 2 * (source % 8) + source // 8
        columns = slice(head * DH, (head + 1) * DH)
        wide = parts_ref[source].astype(F32) * scale * gain_ref[:, columns][None]
        out_ref[:, :, columns] = wide.astype(BF)


PARAMS = pltpu.CompilerParams(vmem_limit_bytes=16 * 1024 * 1024)
VMEM = pl.BlockSpec(memory_space=pltpu.VMEM)
ANY = pl.BlockSpec(memory_space=pl.ANY)
HBM = pl.BlockSpec(memory_space=pltpu.HBM)
SMEM = pl.BlockSpec(memory_space=pltpu.SMEM)


def shape_of(shape, dtype=BF):
    return jax.ShapeDtypeStruct(shape, dtype)


def body(queries, keys, values, token_rates, step_size, w_gate, w_up, w_down, norm_gain):
    core = lax.axis_index("core")
    chip = lax.axis_index(RING).astype(jnp.int32).reshape(1)
    line = lax.axis_index("y_hi").astype(jnp.int32).reshape(1)
    pieces = (queries, keys, values, token_rates, w_gate, w_up, w_down)
    place = core.astype(jnp.int32).reshape(1)
    mine, other, dealt = pl.pallas_call(
        pack_kernel,
        out_shape=(shape_of((392, DH)), shape_of((392, DH)), shape_of((64, 24, DH))),
        in_specs=[SMEM] + [HBM] * 7,
        out_specs=(VMEM,) * 3,
        scratch_shapes=[pltpu.VMEM(piece.shape, piece.dtype) for piece in pieces]
        + [pltpu.SemaphoreType.DMA((7,))],
        compiler_params=pltpu.CompilerParams(vmem_limit_bytes=61500 * 1024),
        name="pack",
    )(place, *pieces)
    dealt = lax.all_to_all(dealt, RING + ("core",), 0, 0, tiled=True)
    arrived = lax.ppermute(other, "core", [(0, 1), (1, 0)])
    own, context, pool = pl.pallas_call(
        arrange_kernel,
        out_shape=(shape_of((2, 392, DH)), shape_of((2, 256, DH)), shape_of((272, DH))),
        in_specs=[SMEM, VMEM, VMEM],
        out_specs=(VMEM,) * 3,
        compiler_params=PARAMS,
        name="arrange",
    )(place, mine, arrived)
    pools = [pool]
    for distance in range(1, 4):
        pools.append(lax.ppermute(pool, "y_hi", [(i, (i + distance) % 4) for i in range(4)]))
    ring = [(i, (i + 1) % CHIPS) for i in range(CHIPS)]
    chunks = [lax.ppermute(context, RING, ring)]

    grad, slices, down_fast = pl.pallas_call(
        grad_kernel,
        out_shape=(shape_of((8, 96, PART)), shape_of((4, 2 * DH, PART)), shape_of((DF, DH))),
        in_specs=[SMEM] + [VMEM] * 5,
        out_specs=(VMEM,) * 3,
        compiler_params=PARAMS,
        name="grad",
    )(line, *pools, dealt)
    parts = lax.all_to_all(grad, "z", 0, 0, tiled=True)
    chunks.append(lax.ppermute(chunks[-1], RING, ring))
    total = pl.pallas_call(
        sum_kernel,
        out_shape=shape_of((8, 96, PART)),
        in_specs=[VMEM],
        out_specs=VMEM,
        compiler_params=PARAMS,
        name="sum",
    )(parts)
    total = lax.all_to_all(total, "z", 0, 0, tiled=True)
    chunks.append(lax.ppermute(chunks[-1], RING, ring))
    total = pl.pallas_call(
        widen_kernel,
        out_shape=shape_of((4, 8, 96, PART)),
        in_specs=[VMEM],
        out_specs=VMEM,
        compiler_params=PARAMS,
        name="widen",
    )(total)
    total = lax.all_to_all(total, "y_hi", 0, 0, tiled=True)

    step = lax.dynamic_slice_in_dim(step_size, core, 1, 0)
    fast = pl.pallas_call(
        newton_kernel,
        out_shape=shape_of((TOK, DH), F32),
        in_specs=[SMEM] + [VMEM] * 4 + [ANY],
        out_specs=VMEM,
        scratch_shapes=[pltpu.VMEM((3, DH, DF), F32)],
        compiler_params=PARAMS,
        cost_estimate=pl.CostEstimate(
            flops=8_000_000_000, transcendentals=100_000, bytes_accessed=4_000_000
        ),
        name="newton",
    )(step, total, slices, down_fast, own, chunks[2])
    chunks.append(lax.ppermute(chunks[-1], RING, ring))
    chunks = [chunk.reshape(2, 4, 64, DH) for chunk in chunks]
    combined = pl.pallas_call(
        attention_kernel,
        out_shape=shape_of((16, 2, 8, DH)),
        in_specs=[SMEM] + [VMEM] * 8,
        out_specs=VMEM,
        compiler_params=PARAMS,
        name="window",
    )(chip, own, *chunks, slices, down_fast, fast)
    gathered = lax.all_to_all(combined, ("core", "y_lo", "x"), 0, 0, tiled=True)
    return pl.pallas_call(
        norm_kernel,
        out_shape=jax.ShapeDtypeStruct((2, 8, 16 * DH), BF),
        in_specs=[VMEM] * 2,
        out_specs=VMEM,
        compiler_params=PARAMS,
        name="norm",
    )(gathered, norm_gain.reshape(1, 16 * DH))


def solution(mesh):
    fine = Mesh(mesh.devices.reshape(2, 4, 4, 8, 2), ("y_lo", "x", "y_hi", "z", "core"))
    seq = RING + ("core",)
    head = ("y_lo", "x")
    placed = (
        P(None, seq, head),
        P(None, seq, head),
        P(None, seq, head),
        P(None, head, seq),
        P(head),
        P(head, seq, None),
        P(head, seq, None),
        P(head, seq, None),
        P(),
    )
    return jax.shard_map(
        body, mesh=fine, in_specs=placed, out_specs=P(None, seq + head, None), check_vma=False
    )
```

```python
import math

import jax
import jax.numpy as jnp
from jax import lax
from jax.experimental import pallas as pl
from jax.experimental.pallas import tpu as pltpu
from jax.sharding import Mesh
from jax.sharding import PartitionSpec as P

DH = 256
DF = 512
PART = 128
NS_STEPS = 5
CHIPS = 32
TOK = 128
REACH = 4
RING = ("y_hi", "z")
F32 = jnp.float32
BF = jnp.bfloat16


def matmul(left, right):
    return lax.dot_general(left, right, (((1,), (0,)), ((), ())), preferred_element_type=F32)


def matmul_nt(left, right):
    return lax.dot_general(left, right, (((1,), (1,)), ((), ())), preferred_element_type=F32)


def matmul_tn(left, right):
    return lax.dot_general(left, right, (((0,), (0,)), ((), ())), preferred_element_type=F32)


def halves(wide):
    high = wide.astype(BF)
    return high, (wide - high.astype(F32)).astype(BF)


def rms_norm(values_in):
    wide = values_in.astype(F32)
    mean_square = jnp.mean(wide * wide, axis=-1, keepdims=True)
    return (wide * lax.rsqrt(mean_square + 1e-06)).astype(BF)


def sigmoid(value):
    return 1.0 / (1.0 + jnp.exp(-value))


def fast_forward(query, gate_fast, up_fast, down_fast):
    query_norm = rms_norm(query)
    gate_query = matmul(query_norm, gate_fast)
    up_query = matmul(query_norm, up_fast)
    hidden = (gate_query * sigmoid(gate_query) * up_query).astype(BF)
    return matmul(hidden, down_fast)


def pack_kernel(
    core_ref, q_in, k_in, v_in, rate_in, gate_in, up_in, down_in, mine_ref, other_ref, pool_ref, *scratch
):
    sources = (q_in, k_in, v_in, rate_in, gate_in, up_in, down_in)
    q_ref, k_ref, v_ref, rate_ref, gate_ref, up_ref, down_ref = scratch[:7]
    semaphores = scratch[7]
    copies = [
        pltpu.make_async_copy(source, target, semaphores.at[index])
        for index, (source, target) in enumerate(zip(sources, scratch[:7]))
    ]
    for copy in copies:
        copy.start()
    for copy in copies:
        copy.wait()

    def fill(target, head):
        columns = slice(head * DH, (head + 1) * DH)
        for index, ref in enumerate((q_ref, k_ref, v_ref)):
            for block in range(2):
                first = (index * 2 + block) * 64
                target[first : first + 64, :] = ref[block, :, columns]

    for head in range(2):

        @pl.when(core_ref[0] == head)
        def _():
            fill(mine_ref, head)
            fill(other_ref, 1 - head)

        tiles = []
        for ref in (gate_ref, up_ref):
            wide = ref[head].astype(F32)
            tiles += [wide[:, :DH], wide[:, DH:]]
        tiles.append(down_ref[head].astype(F32))
        weights = jnp.concatenate(tiles, 0).astype(BF)
        rate = rate_ref[0, head : head + 1, :]
        high = rate.astype(BF).astype(F32)
        middle = (rate - high).astype(BF).astype(F32)
        low = (rate - high) - middle
        terms = jnp.concatenate([high, middle, low, jnp.zeros_like(rate)], 1)
        terms = jnp.broadcast_to(terms, (8, DH)).astype(BF)
        columns = slice(head * DH, (head + 1) * DH)
        for row in range(4):
            target = 2 * row + head
            pool_ref[target, 0:64, :] = k_ref[0, :, columns]
            pool_ref[target, 64:128, :] = v_ref[0, :, columns]
            pool_ref[target, 128:136, :] = terms
            pool_ref[target, 136:160, :] = weights


def regroup_kernel(pool_ref, deal_ref):
    for source in range(8):
        piece = pool_ref[source, 136:160, :]
        for depth in range(8):
            deal_ref[depth, 24 * source : 24 * source + 24, :] = piece


def arrange_kernel(core_ref, mine_ref, arrived_ref, own_ref, context_ref):
    own_ref[core_ref[0]] = mine_ref[...]
    own_ref[1 - core_ref[0]] = arrived_ref[...]
    for source in range(2):
        context_ref[source] = own_ref[source, 128:384, :]


def grad_kernel(row_ref, pool_ref, raw_ref, grad_ref, slices_ref, down_ref):
    out_row = lax.broadcasted_iota(jnp.int32, (DH, 2 * DH), 0)
    in_row = lax.broadcasted_iota(jnp.int32, (DH, 2 * DH), 1)
    sender = out_row // 4
    order = (sender % 16 // 2) * 8 + (sender // 16) * 2 + sender % 2
    pick = order * 8 + out_row % 4
    for index in range(2):
        first = 8 * index
        starts = [24 * source + first for source in range(8)]
        pieces = [raw_ref[:, start : start + 8, :].astype(F32) for start in starts]
        mixed = jnp.stack(pieces, 1).reshape(2 * DH, DH).astype(BF)
        rows = slice(index * DH, (index + 1) * DH)
        for half in range(2):
            chosen = jnp.where(in_row == pick + 4 * half, 1.0, 0.0).astype(BF)
            ordered = matmul(chosen, mixed).astype(BF)
            slices_ref[2 * half, rows, :] = ordered[:, :PART]
            slices_ref[2 * half + 1, rows, :] = ordered[:, PART:]
    for y in range(4):
        starts = [24 * (2 * y + source) + 16 for source in range(2)]
        pieces = [raw_ref[:, start : start + 8, :].astype(F32) for start in starts]
        down_ref[PART * y : PART * (y + 1), :] = jnp.stack(pieces, 1).reshape(PART, DH).astype(BF)
    row = row_ref[0]
    weights = (slices_ref[row, :DH, :], slices_ref[row, DH:, :])
    down_part = down_ref[pl.ds(pl.multiple_of(row * PART, PART), PART), :]
    equal = lax.broadcasted_iota(jnp.int32, (64, 64), 0) == lax.broadcasted_iota(
        jnp.int32, (64, 64), 1
    )
    columns = []
    for source in range(8):
        terms = pool_ref[source, 128:136, :].astype(F32)[0:1]
        rate = terms[:, 0:64] + (terms[:, 64:128] + terms[:, 128:192])
        spread = jnp.where(equal, jnp.broadcast_to(rate, (64, 64)), 0.0)
        columns.append(jnp.sum(spread, axis=1, keepdims=True))
    rate_col = jnp.concatenate(columns, 0)
    gate_part, up_part = weights
    keys_now = rms_norm(pool_ref[:, 0:64, :].reshape(4 * TOK, DH))
    vals_now = pool_ref[:, 64:128, :].reshape(4 * TOK, DH)
    gate_pre = matmul(keys_now, gate_part)
    up_pre = matmul(keys_now, up_part)
    back = matmul_nt(vals_now, down_part)
    sigmoid_val = sigmoid(gate_pre)
    act_val = gate_pre * sigmoid_val
    rate_back = rate_col * back
    d_gate = (rate_back * up_pre * sigmoid_val * (1.0 + gate_pre * (1.0 - sigmoid_val))).astype(BF)
    d_up = (rate_back * act_val).astype(BF)
    h_rate = (rate_col * act_val * up_pre).astype(BF)
    for index, (left, right) in enumerate(
        ((keys_now, d_gate), (keys_now, d_up), (vals_now, h_rate))
    ):
        grad = matmul_tn(left, right).reshape(8, 32, PART)
        grad_ref[:, index * 32 : index * 32 + 32, :] = grad.astype(BF)


def sum_kernel(parts_ref, total_ref):
    total = jnp.sum(parts_ref[...].astype(F32), axis=0, keepdims=True)
    total_ref[...] = jnp.broadcast_to(total, (8, 96, PART)).astype(BF)


def widen_kernel(piece_ref, total_ref):
    for row in range(4):
        total_ref[row] = piece_ref[...]


def whole_weights(slices_ref):
    gate_fast = jnp.concatenate([slices_ref[row, :DH, :] for row in range(4)], 1)
    up_fast = jnp.concatenate([slices_ref[row, DH:, :] for row in range(4)], 1)
    return gate_fast, up_fast


def attention_kernel(
    chip_ref, own_ref, c1_ref, c2_ref, c3_ref, c4_ref, slices_ref, down_ref, out_ref
):
    chip = chip_ref[0]
    row = lax.broadcasted_iota(jnp.int32, (TOK, TOK), 0)
    column = lax.broadcasted_iota(jnp.int32, (TOK, TOK), 1)
    scale = 1.0 / math.sqrt(DH)
    chunks = (c1_ref, c2_ref, c3_ref, c4_ref)

    def rows_of(distance, index, block):
        if distance == 0:
            first = (2 + 2 * index + block) * 64
            return jnp.concatenate([own_ref[src, first : first + 64, :] for src in range(2)], 0)
        behind = (chip < distance).astype(jnp.int32)
        place = 2 * index + jnp.maximum(block - behind, 0)
        chunk = chunks[distance - 1]
        return jnp.concatenate([chunk[0, place], chunk[1, place]], 0)

    for block in range(2):
        rows = slice(block * 64, block * 64 + 64)
        query = jnp.concatenate([own_ref[0, rows, :], own_ref[1, rows, :]], 0)
        scores = []
        for distance in range(REACH + 1):
            score = matmul_nt(query, rows_of(distance, 0, block)) * scale
            if distance == 0:
                score = jnp.where(row >= column, score, -1e30)
            elif distance == REACH:
                score = jnp.where(row < column, score, -1e30)
            if block == 0 and distance > 0:
                behind = (chip < distance).astype(jnp.int32)
                score = jnp.where(behind + jnp.zeros_like(row) > 0, -1e30, score)
            scores.append(score)
        top = scores[0]
        for score in scores[1:]:
            top = jnp.maximum(top, score)
        row_top = jnp.max(top, axis=-1, keepdims=True)
        exps = [jnp.exp(score - row_top) for score in scores]
        total = exps[0]
        for exp_score in exps[1:]:
            total = total + exp_score
        row_sum = jnp.sum(total, axis=-1, keepdims=True)
        result = None
        for distance in range(REACH + 1):
            weights = (exps[distance] / row_sum).astype(BF)
            part = matmul(weights, rows_of(distance, 1, block))
            result = part if result is None else result + part
        if block == 0:
            result = result + fast_forward(query, *whole_weights(slices_ref), down_ref[...])
        out_ref[block] = result


def coarse_step(iterates):
    highs = [iterate.astype(BF) for iterate in iterates]
    grams = [matmul_nt(high, high) for high in highs]
    squares = [matmul(gram.astype(BF), gram.astype(BF)) for gram in grams]
    polys = [-4.775 * gram + 2.0315 * square for gram, square in zip(grams, squares)]
    changes = [matmul(poly.astype(BF), high) for poly, high in zip(polys, highs)]
    return [3.4445 * iterate + change for iterate, change in zip(iterates, changes)]


def thrice(left, right, axis):
    left = jnp.concatenate([left[0], left[0], left[1]], 1)
    return left, jnp.concatenate([right[0], right[1], right[0]], axis)


def fine_step(iterates):
    parts = [halves(iterate) for iterate in iterates]
    grams = [matmul_nt(*thrice(part, part, 1)) for part in parts]
    gram_parts = [halves(gram) for gram in grams]
    squares = [matmul(*thrice(part, part, 0)) for part in gram_parts]
    polys = [halves(-4.775 * gram + 2.0315 * square) for gram, square in zip(grams, squares)]
    changes = [matmul(*thrice(poly, part, 0)) for poly, part in zip(polys, parts)]
    return [3.4445 * iterate + change for iterate, change in zip(iterates, changes)]


def newton_kernel(
    step_ref, total_ref, slices_ref, down_ref, own_ref, base_ref, out_ref, iterate_ref
):
    for index in range(3):
        rows = slice(index * 32, index * 32 + 32)
        pieces = [total_ref[row, :, rows, :].astype(F32).reshape(DH, PART) for row in range(4)]
        grad = jnp.concatenate(pieces, 1)
        square = jnp.sum(jnp.sum(grad * grad, axis=0, keepdims=True), axis=1, keepdims=True)
        iterate_ref[index] = grad / (jnp.sqrt(square) + 1e-07)

    iterates = [iterate_ref[index] for index in range(3)]
    for step_index in range(NS_STEPS):
        iterates = coarse_step(iterates) if step_index < 2 else fine_step(iterates)
        for index in range(3):
            iterate_ref[index] = iterates[index]
        iterates = [iterate_ref[index] for index in range(3)]
    step = step_ref[0]
    gate_fast, up_fast = whole_weights(slices_ref)
    gate_fast = (gate_fast.astype(F32) + step * iterate_ref[0]).astype(BF)
    up_fast = (up_fast.astype(F32) + step * iterate_ref[1]).astype(BF)
    down_fast = (down_ref[...].astype(F32) + step * iterate_ref[2].T).astype(BF)
    query = jnp.concatenate([own_ref[0, 64:128, :], own_ref[1, 64:128, :]], 0)
    fast = fast_forward(query, gate_fast, up_fast, down_fast)
    out_ref[:, 0] = base_ref[0].reshape(16, 8, DH).astype(BF)
    out_ref[:, 1] = (fast + base_ref[1]).reshape(16, 8, DH).astype(BF)


def norm_kernel(parts_ref, gain_ref, out_ref):
    square = None
    for source in range(16):
        wide = parts_ref[source].astype(F32)
        part = jnp.sum(wide * wide, axis=-1, keepdims=True)
        square = part if square is None else square + part
    scale = lax.rsqrt(square * (1.0 / (16 * DH)) + 1e-06)
    for source in range(16):
        head = 2 * (source % 8) + source // 8
        columns = slice(head * DH, (head + 1) * DH)
        wide = parts_ref[source].astype(F32) * scale * gain_ref[:, columns][None]
        out_ref[:, :, columns] = wide.astype(BF)


PARAMS = pltpu.CompilerParams(vmem_limit_bytes=16 * 1024 * 1024)
VMEM = pl.BlockSpec(memory_space=pltpu.VMEM)
ANY = pl.BlockSpec(memory_space=pl.ANY)
HBM = pl.BlockSpec(memory_space=pltpu.HBM)
SMEM = pl.BlockSpec(memory_space=pltpu.SMEM)


def shape_of(shape, dtype=BF):
    return jax.ShapeDtypeStruct(shape, dtype)


def body(queries, keys, values, token_rates, step_size, w_gate, w_up, w_down, norm_gain):
    core = lax.axis_index("core")
    chip = lax.axis_index(RING).astype(jnp.int32).reshape(1)
    line = lax.axis_index("y_hi").astype(jnp.int32).reshape(1)
    pieces = (queries, keys, values, token_rates, w_gate, w_up, w_down)
    place = core.astype(jnp.int32).reshape(1)
    mine, other, pool = pl.pallas_call(
        pack_kernel,
        out_shape=(shape_of((384, DH)), shape_of((384, DH)), shape_of((8, 160, DH))),
        in_specs=[SMEM] + [HBM] * 7,
        out_specs=(VMEM,) * 3,
        scratch_shapes=[pltpu.VMEM(piece.shape, piece.dtype) for piece in pieces]
        + [pltpu.SemaphoreType.DMA((7,))],
        compiler_params=pltpu.CompilerParams(vmem_limit_bytes=61500 * 1024),
        name="pack",
    )(place, *pieces)
    pool = lax.all_to_all(pool, ("y_hi", "core"), 0, 0, tiled=True)
    arrived = lax.ppermute(other, "core", [(0, 1), (1, 0)])
    dealt = pl.pallas_call(
        regroup_kernel,
        out_shape=shape_of((8, 192, DH)),
        in_specs=[VMEM],
        out_specs=VMEM,
        compiler_params=PARAMS,
        name="regroup",
    )(pool)
    dealt = lax.all_to_all(dealt, "z", 0, 0, tiled=True)
    own, context = pl.pallas_call(
        arrange_kernel,
        out_shape=(shape_of((2, 384, DH)), shape_of((2, 256, DH))),
        in_specs=[SMEM, VMEM, VMEM],
        out_specs=(VMEM,) * 2,
        compiler_params=PARAMS,
        name="arrange",
    )(place, mine, arrived)
    ring = [(i, (i + 1) % CHIPS) for i in range(CHIPS)]
    chunks = [context]
    for _ in range(1, REACH + 1):
        chunks.append(lax.ppermute(chunks[-1], RING, ring))
    chunks = [chunk.reshape(2, 4, 64, DH) for chunk in chunks[1:]]

    grad, slices, down_fast = pl.pallas_call(
        grad_kernel,
        out_shape=(shape_of((8, 96, PART)), shape_of((4, 2 * DH, PART)), shape_of((DF, DH))),
        in_specs=[SMEM] + [VMEM] * 2,
        out_specs=(VMEM,) * 3,
        compiler_params=PARAMS,
        name="grad",
    )(line, pool, dealt)
    parts = lax.all_to_all(grad, "z", 0, 0, tiled=True)
    total = pl.pallas_call(
        sum_kernel,
        out_shape=shape_of((8, 96, PART)),
        in_specs=[VMEM],
        out_specs=VMEM,
        compiler_params=PARAMS,
        name="sum",
    )(parts)
    total = lax.all_to_all(total, "z", 0, 0, tiled=True)
    total = pl.pallas_call(
        widen_kernel,
        out_shape=shape_of((4, 8, 96, PART)),
        in_specs=[VMEM],
        out_specs=VMEM,
        compiler_params=PARAMS,
        name="widen",
    )(total)
    total = lax.all_to_all(total, "y_hi", 0, 0, tiled=True)

    base = pl.pallas_call(
        attention_kernel,
        out_shape=shape_of((2, TOK, DH), F32),
        in_specs=[SMEM] + [VMEM] * 7,
        out_specs=VMEM,
        compiler_params=PARAMS,
        name="window",
    )(chip, own, *chunks, slices, down_fast)
    step = lax.dynamic_slice_in_dim(step_size, core, 1, 0)
    combined = pl.pallas_call(
        newton_kernel,
        out_shape=shape_of((16, 2, 8, DH)),
        in_specs=[SMEM] + [VMEM] * 5,
        out_specs=VMEM,
        scratch_shapes=[pltpu.VMEM((3, DH, DF), F32)],
        compiler_params=PARAMS,
        name="newton",
    )(step, total, slices, down_fast, own, base)
    gathered = lax.all_to_all(combined, ("core", "y_lo", "x"), 0, 0, tiled=True)
    return pl.pallas_call(
        norm_kernel,
        out_shape=jax.ShapeDtypeStruct((2, 8, 16 * DH), BF),
        in_specs=[VMEM] * 2,
        out_specs=VMEM,
        compiler_params=PARAMS,
        name="norm",
    )(gathered, norm_gain.reshape(1, 16 * DH))


def solution(mesh):
    fine = Mesh(mesh.devices.reshape(2, 4, 4, 8, 2), ("y_lo", "x", "y_hi", "z", "core"))
    seq = RING + ("core",)
    head = ("y_lo", "x")
    placed = (
        P(None, seq, head),
        P(None, seq, head),
        P(None, seq, head),
        P(None, head, seq),
        P(head),
        P(head, seq, None),
        P(head, seq, None),
        P(head, seq, None),
        P(),
    )
    return jax.shard_map(
        body, mesh=fine, in_specs=placed, out_specs=P(None, seq + head, None), check_vma=False
    )
```

```python
import math

import jax
import jax.numpy as jnp
from jax import lax
from jax.experimental import pallas as pl
from jax.experimental.pallas import tpu as pltpu
from jax.sharding import Mesh
from jax.sharding import PartitionSpec as P

DH = 256
DF = 512
PART = 128
NS_STEPS = 5
CHIPS = 32
TOK = 128
REACH = 4
RING = ("y_hi", "z")
F32 = jnp.float32
BF = jnp.bfloat16


def matmul(left, right):
    return lax.dot_general(left, right, (((1,), (0,)), ((), ())), preferred_element_type=F32)


def matmul_nt(left, right):
    return lax.dot_general(left, right, (((1,), (1,)), ((), ())), preferred_element_type=F32)


def matmul_tn(left, right):
    return lax.dot_general(left, right, (((0,), (0,)), ((), ())), preferred_element_type=F32)


def halves(wide):
    high = wide.astype(BF)
    return high, (wide - high.astype(F32)).astype(BF)


def rms_norm(values_in):
    wide = values_in.astype(F32)
    mean_square = jnp.mean(wide * wide, axis=-1, keepdims=True)
    return (wide * lax.rsqrt(mean_square + 1e-06)).astype(BF)


def sigmoid(value):
    return 1.0 / (1.0 + jnp.exp(-value))


def fast_forward(query, gate_fast, up_fast, down_fast):
    query_norm = rms_norm(query)
    gate_query = matmul(query_norm, gate_fast)
    up_query = matmul(query_norm, up_fast)
    hidden = (gate_query * sigmoid(gate_query) * up_query).astype(BF)
    return matmul(hidden, down_fast)


def pack_kernel(
    core_ref, q_in, k_in, v_in, rate_in, gate_in, up_in, down_in, mine_ref, other_ref, deal_ref, *scratch
):
    sources = (q_in, k_in, v_in, rate_in, gate_in, up_in, down_in)
    q_ref, k_ref, v_ref, rate_ref, gate_ref, up_ref, down_ref = scratch[:7]
    semaphores = scratch[7]
    copies = [
        pltpu.make_async_copy(source, target, semaphores.at[index])
        for index, (source, target) in enumerate(zip(sources, scratch[:7]))
    ]
    for copy in copies:
        copy.start()
    for copy in copies:
        copy.wait()

    def fill(target, head):
        columns = slice(head * DH, (head + 1) * DH)
        for index, ref in enumerate((q_ref, k_ref, v_ref)):
            for block in range(2):
                first = (index * 2 + block) * 64
                target[first : first + 64, :] = ref[block, :, columns]
        rate = rate_ref[0, head : head + 1, :]
        high = rate.astype(BF).astype(F32)
        middle = (rate - high).astype(BF).astype(F32)
        low = (rate - high) - middle
        terms = jnp.concatenate([high, middle, low, jnp.zeros_like(rate)], 1)
        target[384:392, :] = jnp.broadcast_to(terms, (8, DH)).astype(BF)

    for head in range(2):

        @pl.when(core_ref[0] == head)
        def _():
            fill(mine_ref, head)
            fill(other_ref, 1 - head)

        tiles = []
        for ref in (gate_ref, up_ref):
            wide = ref[head].astype(F32)
            tiles += [wide[:, :DH], wide[:, DH:]]
        tiles.append(down_ref[head].astype(F32))
        piece = jnp.concatenate(tiles, 0).astype(BF)
        for row in range(4):
            deal_ref[row, 24 * head : 24 * head + 24, :] = piece


def regroup_kernel(rows_ref, deal_ref):
    for head in range(2):
        for row in range(4):
            piece = rows_ref[row, 24 * head : 24 * head + 24, :]
            for depth in range(8):
                deal_ref[2 * depth + head, 24 * row : 24 * row + 24, :] = piece


def arrange_kernel(core_ref, mine_ref, arrived_ref, own_ref, context_ref, pool_ref):
    own_ref[core_ref[0]] = mine_ref[...]
    own_ref[1 - core_ref[0]] = arrived_ref[...]
    for source in range(2):
        context_ref[source] = own_ref[source, 128:384, :]
        for index in range(2):
            first = 128 * index + 64 * source
            rows = slice(128 * (index + 1), 128 * (index + 1) + 64)
            pool_ref[first : first + 64, :] = own_ref[source, rows, :]
        pool_ref[256 + 8 * source : 264 + 8 * source, :] = own_ref[source, 384:392, :]


def grad_kernel(row_ref, p0_ref, p1_ref, p2_ref, p3_ref, raw_ref, grad_ref, slices_ref, down_ref):
    pools = (p0_ref, p1_ref, p2_ref, p3_ref)
    out_row = lax.broadcasted_iota(jnp.int32, (DH, 2 * DH), 0)
    in_row = lax.broadcasted_iota(jnp.int32, (DH, 2 * DH), 1)
    sender = out_row // 4
    pick = (sender % 16) * 32 + (sender // 16) * 8 + out_row % 4
    for index in range(2):
        first = 8 * index
        pieces = [raw_ref[:, 24 * y + first : 24 * y + first + 8, :].astype(F32) for y in range(4)]
        mixed = jnp.stack(pieces, 1).reshape(2 * DH, DH).astype(BF)
        rows = slice(index * DH, (index + 1) * DH)
        for half in range(2):
            chosen = jnp.where(in_row == pick + 4 * half, 1.0, 0.0).astype(BF)
            ordered = matmul(chosen, mixed).astype(BF)
            slices_ref[2 * half, rows, :] = ordered[:, :PART]
            slices_ref[2 * half + 1, rows, :] = ordered[:, PART:]
    for y in range(4):
        piece = raw_ref[:, 24 * y + 16 : 24 * y + 24, :].astype(F32).reshape(PART, DH)
        down_ref[PART * y : PART * (y + 1), :] = piece.astype(BF)
    row = row_ref[0]
    weights = (slices_ref[row, :DH, :], slices_ref[row, DH:, :])
    down_part = down_ref[pl.ds(pl.multiple_of(row * PART, PART), PART), :]
    equal = lax.broadcasted_iota(jnp.int32, (64, 64), 0) == lax.broadcasted_iota(
        jnp.int32, (64, 64), 1
    )
    columns = []
    for pool in pools:
        for source in range(2):
            terms = pool[256 + 8 * source : 264 + 8 * source, :].astype(F32)[0:1]
            rate = terms[:, 0:64] + (terms[:, 64:128] + terms[:, 128:192])
            spread = jnp.where(equal, jnp.broadcast_to(rate, (64, 64)), 0.0)
            columns.append(jnp.sum(spread, axis=1, keepdims=True))
    rate_col = jnp.concatenate(columns, 0)
    gate_part, up_part = weights
    keys_now = rms_norm(jnp.concatenate([pool[0:128, :] for pool in pools], 0))
    vals_now = jnp.concatenate([pool[128:256, :] for pool in pools], 0)
    gate_pre = matmul(keys_now, gate_part)
    up_pre = matmul(keys_now, up_part)
    back = matmul_nt(vals_now, down_part)
    sigmoid_val = sigmoid(gate_pre)
    act_val = gate_pre * sigmoid_val
    rate_back = rate_col * back
    d_gate = (rate_back * up_pre * sigmoid_val * (1.0 + gate_pre * (1.0 - sigmoid_val))).astype(BF)
    d_up = (rate_back * act_val).astype(BF)
    h_rate = (rate_col * act_val * up_pre).astype(BF)
    for index, (left, right) in enumerate(
        ((keys_now, d_gate), (keys_now, d_up), (vals_now, h_rate))
    ):
        grad = matmul_tn(left, right).reshape(8, 32, PART)
        grad_ref[:, index * 32 : index * 32 + 32, :] = grad.astype(BF)


def sum_kernel(parts_ref, total_ref):
    total = jnp.sum(parts_ref[...].astype(F32), axis=0, keepdims=True)
    total_ref[...] = jnp.broadcast_to(total, (8, 96, PART)).astype(BF)


def widen_kernel(piece_ref, total_ref):
    for row in range(4):
        total_ref[row] = piece_ref[...]


def whole_weights(slices_ref):
    gate_fast = jnp.concatenate([slices_ref[row, :DH, :] for row in range(4)], 1)
    up_fast = jnp.concatenate([slices_ref[row, DH:, :] for row in range(4)], 1)
    return gate_fast, up_fast


def attention_kernel(
    chip_ref, own_ref, c1_ref, c2_ref, c3_ref, c4_ref, slices_ref, down_ref, fast_ref, out_ref
):
    chip = chip_ref[0]
    row = lax.broadcasted_iota(jnp.int32, (TOK, TOK), 0)
    column = lax.broadcasted_iota(jnp.int32, (TOK, TOK), 1)
    scale = 1.0 / math.sqrt(DH)
    chunks = (c1_ref, c2_ref, c3_ref, c4_ref)

    def rows_of(distance, index, block):
        if distance == 0:
            first = (2 + 2 * index + block) * 64
            return jnp.concatenate([own_ref[src, first : first + 64, :] for src in range(2)], 0)
        behind = (chip < distance).astype(jnp.int32)
        place = 2 * index + jnp.maximum(block - behind, 0)
        chunk = chunks[distance - 1]
        return jnp.concatenate([chunk[0, place], chunk[1, place]], 0)

    for block in range(2):
        rows = slice(block * 64, block * 64 + 64)
        query = jnp.concatenate([own_ref[0, rows, :], own_ref[1, rows, :]], 0)
        scores = []
        for distance in range(REACH + 1):
            score = matmul_nt(query, rows_of(distance, 0, block)) * scale
            if distance == 0:
                score = jnp.where(row >= column, score, -1e30)
            elif distance == REACH:
                score = jnp.where(row < column, score, -1e30)
            if block == 0 and distance > 0:
                behind = (chip < distance).astype(jnp.int32)
                score = jnp.where(behind + jnp.zeros_like(row) > 0, -1e30, score)
            scores.append(score)
        top = scores[0]
        for score in scores[1:]:
            top = jnp.maximum(top, score)
        row_top = jnp.max(top, axis=-1, keepdims=True)
        exps = [jnp.exp(score - row_top) for score in scores]
        total = exps[0]
        for exp_score in exps[1:]:
            total = total + exp_score
        row_sum = jnp.sum(total, axis=-1, keepdims=True)
        result = None
        for distance in range(REACH + 1):
            weights = (exps[distance] / row_sum).astype(BF)
            part = matmul(weights, rows_of(distance, 1, block))
            result = part if result is None else result + part
        if block == 0:
            result = result + fast_forward(query, *whole_weights(slices_ref), down_ref[...])
        else:
            result = result + fast_ref[...]
        out_ref[:, block] = result.reshape(16, 8, DH).astype(BF)


def coarse_step(iterates):
    highs = [iterate.astype(BF) for iterate in iterates]
    grams = [matmul_nt(high, high) for high in highs]
    squares = [matmul(gram.astype(BF), gram.astype(BF)) for gram in grams]
    polys = [-4.775 * gram + 2.0315 * square for gram, square in zip(grams, squares)]
    changes = [matmul(poly.astype(BF), high) for poly, high in zip(polys, highs)]
    return [3.4445 * iterate + change for iterate, change in zip(iterates, changes)]


def thrice(left, right, axis):
    left = jnp.concatenate([left[0], left[0], left[1]], 1)
    return left, jnp.concatenate([right[0], right[1], right[0]], axis)


def fine_step(iterates):
    parts = [halves(iterate) for iterate in iterates]
    grams = [matmul_nt(*thrice(part, part, 1)) for part in parts]
    gram_parts = [halves(gram) for gram in grams]
    squares = [matmul(*thrice(part, part, 0)) for part in gram_parts]
    polys = [halves(-4.775 * gram + 2.0315 * square) for gram, square in zip(grams, squares)]
    changes = [matmul(*thrice(poly, part, 0)) for poly, part in zip(polys, parts)]
    return [3.4445 * iterate + change for iterate, change in zip(iterates, changes)]


def newton_kernel(
    step_ref, total_ref, slices_ref, down_ref, own_ref, _, fast_ref, iterate_ref
):
    for index in range(3):
        rows = slice(index * 32, index * 32 + 32)
        pieces = [total_ref[row, :, rows, :].astype(F32).reshape(DH, PART) for row in range(4)]
        grad = jnp.concatenate(pieces, 1)
        square = jnp.sum(jnp.sum(grad * grad, axis=0, keepdims=True), axis=1, keepdims=True)
        iterate_ref[index] = grad / (jnp.sqrt(square) + 1e-07)

    iterates = [iterate_ref[index] for index in range(3)]
    for step_index in range(NS_STEPS):
        iterates = coarse_step(iterates) if step_index < 2 else fine_step(iterates)
        for index in range(3):
            iterate_ref[index] = iterates[index]
        iterates = [iterate_ref[index] for index in range(3)]
    step = step_ref[0]
    gate_fast, up_fast = whole_weights(slices_ref)
    gate_fast = (gate_fast.astype(F32) + step * iterate_ref[0]).astype(BF)
    up_fast = (up_fast.astype(F32) + step * iterate_ref[1]).astype(BF)
    down_fast = (down_ref[...].astype(F32) + step * iterate_ref[2].T).astype(BF)
    query = jnp.concatenate([own_ref[0, 64:128, :], own_ref[1, 64:128, :]], 0)
    fast_ref[...] = fast_forward(query, gate_fast, up_fast, down_fast)


def norm_kernel(parts_ref, gain_ref, out_ref):
    square = None
    for source in range(16):
        wide = parts_ref[source].astype(F32)
        part = jnp.sum(wide * wide, axis=-1, keepdims=True)
        square = part if square is None else square + part
    scale = lax.rsqrt(square * (1.0 / (16 * DH)) + 1e-06)
    for source in range(16):
        head = 2 * (source % 8) + source // 8
        columns = slice(head * DH, (head + 1) * DH)
        wide = parts_ref[source].astype(F32) * scale * gain_ref[:, columns][None]
        out_ref[:, :, columns] = wide.astype(BF)


PARAMS = pltpu.CompilerParams(vmem_limit_bytes=16 * 1024 * 1024)
VMEM = pl.BlockSpec(memory_space=pltpu.VMEM)
ANY = pl.BlockSpec(memory_space=pl.ANY)
HBM = pl.BlockSpec(memory_space=pltpu.HBM)
SMEM = pl.BlockSpec(memory_space=pltpu.SMEM)


def shape_of(shape, dtype=BF):
    return jax.ShapeDtypeStruct(shape, dtype)


def body(queries, keys, values, token_rates, step_size, w_gate, w_up, w_down, norm_gain):
    core = lax.axis_index("core")
    chip = lax.axis_index(RING).astype(jnp.int32).reshape(1)
    line = lax.axis_index("y_hi").astype(jnp.int32).reshape(1)
    pieces = (queries, keys, values, token_rates, w_gate, w_up, w_down)
    place = core.astype(jnp.int32).reshape(1)
    mine, other, dealt = pl.pallas_call(
        pack_kernel,
        out_shape=(shape_of((392, DH)), shape_of((392, DH)), shape_of((4, 48, DH))),
        in_specs=[SMEM] + [HBM] * 7,
        out_specs=(VMEM,) * 3,
        scratch_shapes=[pltpu.VMEM(piece.shape, piece.dtype) for piece in pieces]
        + [pltpu.SemaphoreType.DMA((7,))],
        compiler_params=pltpu.CompilerParams(vmem_limit_bytes=61500 * 1024),
        name="pack",
    )(place, *pieces)
    dealt = lax.all_to_all(dealt, "y_hi", 0, 0, tiled=True)
    dealt = pl.pallas_call(
        regroup_kernel,
        out_shape=shape_of((16, 96, DH)),
        in_specs=[VMEM],
        out_specs=VMEM,
        compiler_params=PARAMS,
        name="regroup",
    )(dealt)
    dealt = lax.all_to_all(dealt, ("z", "core"), 0, 0, tiled=True)
    arrived = lax.ppermute(other, "core", [(0, 1), (1, 0)])
    own, context, pool = pl.pallas_call(
        arrange_kernel,
        out_shape=(shape_of((2, 392, DH)), shape_of((2, 256, DH)), shape_of((272, DH))),
        in_specs=[SMEM, VMEM, VMEM],
        out_specs=(VMEM,) * 3,
        compiler_params=PARAMS,
        name="arrange",
    )(place, mine, arrived)
    pools = [pool]
    for distance in range(1, 4):
        pools.append(lax.ppermute(pool, "y_hi", [(i, (i + distance) % 4) for i in range(4)]))
    ring = [(i, (i + 1) % CHIPS) for i in range(CHIPS)]
    chunks = [lax.ppermute(context, RING, ring)]

    grad, slices, down_fast = pl.pallas_call(
        grad_kernel,
        out_shape=(shape_of((8, 96, PART)), shape_of((4, 2 * DH, PART)), shape_of((DF, DH))),
        in_specs=[SMEM] + [VMEM] * 5,
        out_specs=(VMEM,) * 3,
        compiler_params=PARAMS,
        name="grad",
    )(line, *pools, dealt)
    parts = lax.all_to_all(grad, "z", 0, 0, tiled=True)
    chunks.append(lax.ppermute(chunks[-1], RING, ring))
    total = pl.pallas_call(
        sum_kernel,
        out_shape=shape_of((8, 96, PART)),
        in_specs=[VMEM],
        out_specs=VMEM,
        compiler_params=PARAMS,
        name="sum",
    )(parts)
    total = lax.all_to_all(total, "z", 0, 0, tiled=True)
    chunks.append(lax.ppermute(chunks[-1], RING, ring))
    total = pl.pallas_call(
        widen_kernel,
        out_shape=shape_of((4, 8, 96, PART)),
        in_specs=[VMEM],
        out_specs=VMEM,
        compiler_params=PARAMS,
        name="widen",
    )(total)
    total = lax.all_to_all(total, "y_hi", 0, 0, tiled=True)

    step = lax.dynamic_slice_in_dim(step_size, core, 1, 0)
    fast = pl.pallas_call(
        newton_kernel,
        out_shape=shape_of((TOK, DH), F32),
        in_specs=[SMEM] + [VMEM] * 4 + [ANY],
        out_specs=VMEM,
        scratch_shapes=[pltpu.VMEM((3, DH, DF), F32)],
        compiler_params=PARAMS,
        cost_estimate=pl.CostEstimate(
            flops=8_000_000_000, transcendentals=100_000, bytes_accessed=4_000_000
        ),
        name="newton",
    )(step, total, slices, down_fast, own, chunks[2])
    chunks.append(lax.ppermute(chunks[-1], RING, ring))
    chunks = [chunk.reshape(2, 4, 64, DH) for chunk in chunks]
    combined = pl.pallas_call(
        attention_kernel,
        out_shape=shape_of((16, 2, 8, DH)),
        in_specs=[SMEM] + [VMEM] * 8,
        out_specs=VMEM,
        compiler_params=PARAMS,
        name="window",
    )(chip, own, *chunks, slices, down_fast, fast)
    gathered = lax.all_to_all(combined, ("core", "y_lo", "x"), 0, 0, tiled=True)
    return pl.pallas_call(
        norm_kernel,
        out_shape=jax.ShapeDtypeStruct((2, 8, 16 * DH), BF),
        in_specs=[VMEM] * 2,
        out_specs=VMEM,
        compiler_params=PARAMS,
        name="norm",
    )(gathered, norm_gain.reshape(1, 16 * DH))


def solution(mesh):
    fine = Mesh(mesh.devices.reshape(2, 4, 4, 8, 2), ("y_lo", "x", "y_hi", "z", "core"))
    seq = RING + ("core",)
    head = ("y_lo", "x")
    placed = (
        P(None, seq, head),
        P(None, seq, head),
        P(None, seq, head),
        P(None, head, seq),
        P(head),
        P(head, seq, None),
        P(head, seq, None),
        P(head, seq, None),
        P(),
    )
    return jax.shard_map(
        body, mesh=fine, in_specs=placed, out_specs=P(None, seq + head, None), check_vma=False
    )
```

```python
import math

import jax
import jax.numpy as jnp
from jax import lax
from jax.experimental import pallas as pl
from jax.experimental.pallas import tpu as pltpu
from jax.sharding import Mesh
from jax.sharding import PartitionSpec as P

DH = 256
DF = 512
PART = 128
NS_STEPS = 5
CHIPS = 32
TOK = 128
REACH = 4
RING = ("y_hi", "z")
F32 = jnp.float32
BF = jnp.bfloat16


def matmul(left, right):
    return lax.dot_general(left, right, (((1,), (0,)), ((), ())), preferred_element_type=F32)


def matmul_nt(left, right):
    return lax.dot_general(left, right, (((1,), (1,)), ((), ())), preferred_element_type=F32)


def matmul_tn(left, right):
    return lax.dot_general(left, right, (((0,), (0,)), ((), ())), preferred_element_type=F32)


def halves(wide):
    high = wide.astype(BF)
    return high, (wide - high.astype(F32)).astype(BF)


def rms_norm(values_in):
    wide = values_in.astype(F32)
    mean_square = jnp.mean(wide * wide, axis=-1, keepdims=True)
    return (wide * lax.rsqrt(mean_square + 1e-06)).astype(BF)


def sigmoid(value):
    return 1.0 / (1.0 + jnp.exp(-value))


def fast_forward(query, gate_fast, up_fast, down_fast):
    query_norm = rms_norm(query)
    gate_query = matmul(query_norm, gate_fast)
    up_query = matmul(query_norm, up_fast)
    hidden = (gate_query * sigmoid(gate_query) * up_query).astype(BF)
    return matmul(hidden, down_fast)


def pack_kernel(
    core_ref, q_in, k_in, v_in, rate_in, gate_in, up_in, down_in, mine_ref, other_ref, deal_ref, *scratch
):
    sources = (q_in, k_in, v_in, rate_in, gate_in, up_in, down_in)
    q_ref, k_ref, v_ref, rate_ref, gate_ref, up_ref, down_ref = scratch[:7]
    semaphores = scratch[7]
    copies = [
        pltpu.make_async_copy(source, target, semaphores.at[index])
        for index, (source, target) in enumerate(zip(sources, scratch[:7]))
    ]
    for copy in copies:
        copy.start()
    for copy in copies:
        copy.wait()

    def fill(target, head):
        columns = slice(head * DH, (head + 1) * DH)
        for index, ref in enumerate((q_ref, k_ref, v_ref)):
            for block in range(2):
                first = (index * 2 + block) * 64
                target[first : first + 64, :] = ref[block, :, columns]
        rate = rate_ref[0, head : head + 1, :]
        high = rate.astype(BF).astype(F32)
        middle = (rate - high).astype(BF).astype(F32)
        low = (rate - high) - middle
        terms = jnp.concatenate([high, middle, low, jnp.zeros_like(rate)], 1)
        target[384:392, :] = jnp.broadcast_to(terms, (8, DH)).astype(BF)

    for head in range(2):

        @pl.when(core_ref[0] == head)
        def _():
            fill(mine_ref, head)
            fill(other_ref, 1 - head)

        tiles = []
        for ref in (gate_ref, up_ref):
            wide = ref[head].astype(F32)
            tiles += [wide[:, :DH], wide[:, DH:]]
        tiles.append(down_ref[head].astype(F32))
        piece = jnp.concatenate(tiles, 0).astype(BF)
        for row in range(4):
            deal_ref[row, 24 * head : 24 * head + 24, :] = piece


def regroup_kernel(rows_ref, deal_ref):
    for head in range(2):
        for row in range(4):
            piece = rows_ref[row, 24 * head : 24 * head + 24, :]
            for depth in range(8):
                deal_ref[2 * depth + head, 24 * row : 24 * row + 24, :] = piece


def arrange_kernel(core_ref, mine_ref, arrived_ref, own_ref, context_ref, pool_ref):
    own_ref[core_ref[0]] = mine_ref[...]
    own_ref[1 - core_ref[0]] = arrived_ref[...]
    for source in range(2):
        context_ref[source] = own_ref[source, 128:384, :]
        for index in range(2):
            first = 128 * index + 64 * source
            rows = slice(128 * (index + 1), 128 * (index + 1) + 64)
            pool_ref[first : first + 64, :] = own_ref[source, rows, :]
        pool_ref[256 + 8 * source : 264 + 8 * source, :] = own_ref[source, 384:392, :]


def grad_kernel(row_ref, p0_ref, p1_ref, p2_ref, p3_ref, raw_ref, grad_ref, slices_ref, down_ref):
    pools = (p0_ref, p1_ref, p2_ref, p3_ref)
    out_row = lax.broadcasted_iota(jnp.int32, (DH, 2 * DH), 0)
    in_row = lax.broadcasted_iota(jnp.int32, (DH, 2 * DH), 1)
    sender = out_row // 4
    pick = (sender % 16) * 32 + (sender // 16) * 8 + out_row % 4
    for index in range(2):
        first = 8 * index
        pieces = [raw_ref[:, 24 * y + first : 24 * y + first + 8, :].astype(F32) for y in range(4)]
        mixed = jnp.stack(pieces, 1).reshape(2 * DH, DH).astype(BF)
        rows = slice(index * DH, (index + 1) * DH)
        for half in range(2):
            chosen = jnp.where(in_row == pick + 4 * half, 1.0, 0.0).astype(BF)
            ordered = matmul(chosen, mixed).astype(BF)
            slices_ref[2 * half, rows, :] = ordered[:, :PART]
            slices_ref[2 * half + 1, rows, :] = ordered[:, PART:]
    for y in range(4):
        piece = raw_ref[:, 24 * y + 16 : 24 * y + 24, :].astype(F32).reshape(PART, DH)
        down_ref[PART * y : PART * (y + 1), :] = piece.astype(BF)
    row = row_ref[0]
    weights = (slices_ref[row, :DH, :], slices_ref[row, DH:, :])
    down_part = down_ref[pl.ds(pl.multiple_of(row * PART, PART), PART), :]
    equal = lax.broadcasted_iota(jnp.int32, (64, 64), 0) == lax.broadcasted_iota(
        jnp.int32, (64, 64), 1
    )
    columns = []
    for pool in pools:
        for source in range(2):
            terms = pool[256 + 8 * source : 264 + 8 * source, :].astype(F32)[0:1]
            rate = terms[:, 0:64] + (terms[:, 64:128] + terms[:, 128:192])
            spread = jnp.where(equal, jnp.broadcast_to(rate, (64, 64)), 0.0)
            columns.append(jnp.sum(spread, axis=1, keepdims=True))
    rate_col = jnp.concatenate(columns, 0)
    gate_part, up_part = weights
    keys_now = rms_norm(jnp.concatenate([pool[0:128, :] for pool in pools], 0))
    vals_now = jnp.concatenate([pool[128:256, :] for pool in pools], 0)
    gate_pre = matmul(keys_now, gate_part)
    up_pre = matmul(keys_now, up_part)
    back = matmul_nt(vals_now, down_part)
    sigmoid_val = sigmoid(gate_pre)
    act_val = gate_pre * sigmoid_val
    rate_back = rate_col * back
    d_gate = (rate_back * up_pre * sigmoid_val * (1.0 + gate_pre * (1.0 - sigmoid_val))).astype(BF)
    d_up = (rate_back * act_val).astype(BF)
    h_rate = (rate_col * act_val * up_pre).astype(BF)
    for index, (left, right) in enumerate(
        ((keys_now, d_gate), (keys_now, d_up), (vals_now, h_rate))
    ):
        grad = matmul_tn(left, right).reshape(8, 32, PART)
        grad_ref[:, index * 32 : index * 32 + 32, :] = grad.astype(BF)


def sum_kernel(parts_ref, total_ref):
    total = jnp.sum(parts_ref[...].astype(F32), axis=0, keepdims=True)
    total_ref[...] = jnp.broadcast_to(total, (8, 96, PART)).astype(BF)


def widen_kernel(piece_ref, total_ref):
    for row in range(4):
        total_ref[row] = piece_ref[...]


def whole_weights(slices_ref):
    gate_fast = jnp.concatenate([slices_ref[row, :DH, :] for row in range(4)], 1)
    up_fast = jnp.concatenate([slices_ref[row, DH:, :] for row in range(4)], 1)
    return gate_fast, up_fast


def attention_kernel(
    chip_ref, own_ref, c1_ref, c2_ref, c3_ref, c4_ref, slices_ref, down_ref, out_ref
):
    chip = chip_ref[0]
    row = lax.broadcasted_iota(jnp.int32, (TOK, TOK), 0)
    column = lax.broadcasted_iota(jnp.int32, (TOK, TOK), 1)
    scale = 1.0 / math.sqrt(DH)
    chunks = (c1_ref, c2_ref, c3_ref, c4_ref)

    def rows_of(distance, index, block):
        if distance == 0:
            first = (2 + 2 * index + block) * 64
            return jnp.concatenate([own_ref[src, first : first + 64, :] for src in range(2)], 0)
        behind = (chip < distance).astype(jnp.int32)
        place = 2 * index + jnp.maximum(block - behind, 0)
        chunk = chunks[distance - 1]
        return jnp.concatenate([chunk[0, place], chunk[1, place]], 0)

    for block in range(2):
        rows = slice(block * 64, block * 64 + 64)
        query = jnp.concatenate([own_ref[0, rows, :], own_ref[1, rows, :]], 0)
        scores = []
        for distance in range(REACH + 1):
            score = matmul_nt(query, rows_of(distance, 0, block)) * scale
            if distance == 0:
                score = jnp.where(row >= column, score, -1e30)
            elif distance == REACH:
                score = jnp.where(row < column, score, -1e30)
            if block == 0 and distance > 0:
                behind = (chip < distance).astype(jnp.int32)
                score = jnp.where(behind + jnp.zeros_like(row) > 0, -1e30, score)
            scores.append(score)
        top = scores[0]
        for score in scores[1:]:
            top = jnp.maximum(top, score)
        row_top = jnp.max(top, axis=-1, keepdims=True)
        exps = [jnp.exp(score - row_top) for score in scores]
        total = exps[0]
        for exp_score in exps[1:]:
            total = total + exp_score
        row_sum = jnp.sum(total, axis=-1, keepdims=True)
        result = None
        for distance in range(REACH + 1):
            weights = (exps[distance] / row_sum).astype(BF)
            part = matmul(weights, rows_of(distance, 1, block))
            result = part if result is None else result + part
        if block == 0:
            result = result + fast_forward(query, *whole_weights(slices_ref), down_ref[...])
        out_ref[block] = result


def coarse_step(iterates):
    highs = [iterate.astype(BF) for iterate in iterates]
    grams = [matmul_nt(high, high) for high in highs]
    squares = [matmul(gram.astype(BF), gram.astype(BF)) for gram in grams]
    polys = [-4.775 * gram + 2.0315 * square for gram, square in zip(grams, squares)]
    changes = [matmul(poly.astype(BF), high) for poly, high in zip(polys, highs)]
    return [3.4445 * iterate + change for iterate, change in zip(iterates, changes)]


def thrice(left, right, axis):
    left = jnp.concatenate([left[0], left[0], left[1]], 1)
    return left, jnp.concatenate([right[0], right[1], right[0]], axis)


def fine_step(iterates):
    parts = [halves(iterate) for iterate in iterates]
    grams = [matmul_nt(*thrice(part, part, 1)) for part in parts]
    gram_parts = [halves(gram) for gram in grams]
    squares = [matmul(*thrice(part, part, 0)) for part in gram_parts]
    polys = [halves(-4.775 * gram + 2.0315 * square) for gram, square in zip(grams, squares)]
    changes = [matmul(*thrice(poly, part, 0)) for poly, part in zip(polys, parts)]
    return [3.4445 * iterate + change for iterate, change in zip(iterates, changes)]


def newton_kernel(
    step_ref, total_ref, slices_ref, down_ref, own_ref, base_ref, out_ref, iterate_ref
):
    for index in range(3):
        rows = slice(index * 32, index * 32 + 32)
        pieces = [total_ref[row, :, rows, :].astype(F32).reshape(DH, PART) for row in range(4)]
        grad = jnp.concatenate(pieces, 1)
        square = jnp.sum(jnp.sum(grad * grad, axis=0, keepdims=True), axis=1, keepdims=True)
        iterate_ref[index] = grad / (jnp.sqrt(square) + 1e-07)

    iterates = [iterate_ref[index] for index in range(3)]
    for step_index in range(NS_STEPS):
        iterates = coarse_step(iterates) if step_index < 2 else fine_step(iterates)
        for index in range(3):
            iterate_ref[index] = iterates[index]
        iterates = [iterate_ref[index] for index in range(3)]
    step = step_ref[0]
    gate_fast, up_fast = whole_weights(slices_ref)
    gate_fast = (gate_fast.astype(F32) + step * iterate_ref[0]).astype(BF)
    up_fast = (up_fast.astype(F32) + step * iterate_ref[1]).astype(BF)
    down_fast = (down_ref[...].astype(F32) + step * iterate_ref[2].T).astype(BF)
    query = jnp.concatenate([own_ref[0, 64:128, :], own_ref[1, 64:128, :]], 0)
    fast = fast_forward(query, gate_fast, up_fast, down_fast)
    out_ref[:, 0] = base_ref[0].reshape(16, 8, DH).astype(BF)
    out_ref[:, 1] = (fast + base_ref[1]).reshape(16, 8, DH).astype(BF)


def norm_kernel(parts_ref, gain_ref, out_ref):
    square = None
    for source in range(16):
        wide = parts_ref[source].astype(F32)
        part = jnp.sum(wide * wide, axis=-1, keepdims=True)
        square = part if square is None else square + part
    scale = lax.rsqrt(square * (1.0 / (16 * DH)) + 1e-06)
    for source in range(16):
        head = 2 * (source % 8) + source // 8
        columns = slice(head * DH, (head + 1) * DH)
        wide = parts_ref[source].astype(F32) * scale * gain_ref[:, columns][None]
        out_ref[:, :, columns] = wide.astype(BF)


PARAMS = pltpu.CompilerParams(vmem_limit_bytes=16 * 1024 * 1024)
VMEM = pl.BlockSpec(memory_space=pltpu.VMEM)
ANY = pl.BlockSpec(memory_space=pl.ANY)
HBM = pl.BlockSpec(memory_space=pltpu.HBM)
SMEM = pl.BlockSpec(memory_space=pltpu.SMEM)


def shape_of(shape, dtype=BF):
    return jax.ShapeDtypeStruct(shape, dtype)


def body(queries, keys, values, token_rates, step_size, w_gate, w_up, w_down, norm_gain):
    core = lax.axis_index("core")
    chip = lax.axis_index(RING).astype(jnp.int32).reshape(1)
    line = lax.axis_index("y_hi").astype(jnp.int32).reshape(1)
    pieces = (queries, keys, values, token_rates, w_gate, w_up, w_down)
    place = core.astype(jnp.int32).reshape(1)
    mine, other, dealt = pl.pallas_call(
        pack_kernel,
        out_shape=(shape_of((392, DH)), shape_of((392, DH)), shape_of((4, 48, DH))),
        in_specs=[SMEM] + [HBM] * 7,
        out_specs=(VMEM,) * 3,
        scratch_shapes=[pltpu.VMEM(piece.shape, piece.dtype) for piece in pieces]
        + [pltpu.SemaphoreType.DMA((7,))],
        compiler_params=pltpu.CompilerParams(vmem_limit_bytes=61500 * 1024),
        name="pack",
    )(place, *pieces)
    dealt = lax.all_to_all(dealt, "y_hi", 0, 0, tiled=True)
    dealt = pl.pallas_call(
        regroup_kernel,
        out_shape=shape_of((16, 96, DH)),
        in_specs=[VMEM],
        out_specs=VMEM,
        compiler_params=PARAMS,
        name="regroup",
    )(dealt)
    dealt = lax.all_to_all(dealt, ("z", "core"), 0, 0, tiled=True)
    arrived = lax.ppermute(other, "core", [(0, 1), (1, 0)])
    own, context, pool = pl.pallas_call(
        arrange_kernel,
        out_shape=(shape_of((2, 392, DH)), shape_of((2, 256, DH)), shape_of((272, DH))),
        in_specs=[SMEM, VMEM, VMEM],
        out_specs=(VMEM,) * 3,
        compiler_params=PARAMS,
        name="arrange",
    )(place, mine, arrived)
    pools = [pool]
    for distance in range(1, 4):
        pools.append(lax.ppermute(pool, "y_hi", [(i, (i + distance) % 4) for i in range(4)]))
    ring = [(i, (i + 1) % CHIPS) for i in range(CHIPS)]
    chunks = [lax.ppermute(context, RING, ring)]

    grad, slices, down_fast = pl.pallas_call(
        grad_kernel,
        out_shape=(shape_of((8, 96, PART)), shape_of((4, 2 * DH, PART)), shape_of((DF, DH))),
        in_specs=[SMEM] + [VMEM] * 5,
        out_specs=(VMEM,) * 3,
        compiler_params=PARAMS,
        name="grad",
    )(line, *pools, dealt)
    parts = lax.all_to_all(grad, "z", 0, 0, tiled=True)
    chunks.append(lax.ppermute(chunks[-1], RING, ring))
    total = pl.pallas_call(
        sum_kernel,
        out_shape=shape_of((8, 96, PART)),
        in_specs=[VMEM],
        out_specs=VMEM,
        compiler_params=PARAMS,
        name="sum",
    )(parts)
    total = lax.all_to_all(total, "z", 0, 0, tiled=True)
    chunks.append(lax.ppermute(chunks[-1], RING, ring))
    total = pl.pallas_call(
        widen_kernel,
        out_shape=shape_of((4, 8, 96, PART)),
        in_specs=[VMEM],
        out_specs=VMEM,
        compiler_params=PARAMS,
        name="widen",
    )(total)
    total = lax.all_to_all(total, "y_hi", 0, 0, tiled=True)

    chunks.append(lax.ppermute(chunks[-1], RING, ring))
    chunks = [chunk.reshape(2, 4, 64, DH) for chunk in chunks]
    base = pl.pallas_call(
        attention_kernel,
        out_shape=shape_of((2, TOK, DH), F32),
        in_specs=[SMEM] + [VMEM] * 7,
        out_specs=VMEM,
        compiler_params=PARAMS,
        name="window",
    )(chip, own, *chunks, slices, down_fast)
    step = lax.dynamic_slice_in_dim(step_size, core, 1, 0)
    combined = pl.pallas_call(
        newton_kernel,
        out_shape=shape_of((16, 2, 8, DH)),
        in_specs=[SMEM] + [VMEM] * 5,
        out_specs=VMEM,
        scratch_shapes=[pltpu.VMEM((3, DH, DF), F32)],
        compiler_params=PARAMS,
        name="newton",
    )(step, total, slices, down_fast, own, base)
    gathered = lax.all_to_all(combined, ("core", "y_lo", "x"), 0, 0, tiled=True)
    return pl.pallas_call(
        norm_kernel,
        out_shape=jax.ShapeDtypeStruct((2, 8, 16 * DH), BF),
        in_specs=[VMEM] * 2,
        out_specs=VMEM,
        compiler_params=PARAMS,
        name="norm",
    )(gathered, norm_gain.reshape(1, 16 * DH))


def solution(mesh):
    fine = Mesh(mesh.devices.reshape(2, 4, 4, 8, 2), ("y_lo", "x", "y_hi", "z", "core"))
    seq = RING + ("core",)
    head = ("y_lo", "x")
    placed = (
        P(None, seq, head),
        P(None, seq, head),
        P(None, seq, head),
        P(None, head, seq),
        P(head),
        P(head, seq, None),
        P(head, seq, None),
        P(head, seq, None),
        P(),
    )
    return jax.shard_map(
        body, mesh=fine, in_specs=placed, out_specs=P(None, seq + head, None), check_vma=False
    )
```

```python
import math

import jax
import jax.numpy as jnp
from jax import lax
from jax.experimental import pallas as pl
from jax.experimental.pallas import tpu as pltpu
from jax.sharding import Mesh
from jax.sharding import PartitionSpec as P

DH = 256
DF = 512
PART = 128
NS_STEPS = 5
CHIPS = 32
TOK = 128
REACH = 4
RING = ("y_hi", "z")
F32 = jnp.float32
BF = jnp.bfloat16


def matmul(left, right):
    return lax.dot_general(left, right, (((1,), (0,)), ((), ())), preferred_element_type=F32)


def matmul_nt(left, right):
    return lax.dot_general(left, right, (((1,), (1,)), ((), ())), preferred_element_type=F32)


def matmul_tn(left, right):
    return lax.dot_general(left, right, (((0,), (0,)), ((), ())), preferred_element_type=F32)


def halves(wide):
    high = wide.astype(BF)
    return high, (wide - high.astype(F32)).astype(BF)


def rms_norm(values_in):
    wide = values_in.astype(F32)
    mean_square = jnp.mean(wide * wide, axis=-1, keepdims=True)
    return (wide * lax.rsqrt(mean_square + 1e-06)).astype(BF)


def sigmoid(value):
    return 1.0 / (1.0 + jnp.exp(-value))


def fast_forward(query, gate_fast, up_fast, down_fast):
    query_norm = rms_norm(query)
    gate_query = matmul(query_norm, gate_fast)
    up_query = matmul(query_norm, up_fast)
    hidden = (gate_query * sigmoid(gate_query) * up_query).astype(BF)
    return matmul(hidden, down_fast)


def pack_kernel(
    core_ref, q_in, k_in, v_in, rate_in, gate_in, up_in, down_in, mine_ref, other_ref, deal_ref, *scratch
):
    sources = (q_in, k_in, v_in, rate_in, gate_in, up_in, down_in)
    q_ref, k_ref, v_ref, rate_ref, gate_ref, up_ref, down_ref = scratch[:7]
    semaphores = scratch[7]
    copies = [
        pltpu.make_async_copy(source, target, semaphores.at[index])
        for index, (source, target) in enumerate(zip(sources, scratch[:7]))
    ]
    for copy in copies:
        copy.start()
    for copy in copies:
        copy.wait()

    def fill(target, head):
        columns = slice(head * DH, (head + 1) * DH)
        for index, ref in enumerate((q_ref, k_ref, v_ref)):
            for block in range(2):
                first = (index * 2 + block) * 64
                target[first : first + 64, :] = ref[block, :, columns]
        rate = rate_ref[0, head : head + 1, :]
        high = rate.astype(BF).astype(F32)
        middle = (rate - high).astype(BF).astype(F32)
        low = (rate - high) - middle
        terms = jnp.concatenate([high, middle, low, jnp.zeros_like(rate)], 1)
        target[384:392, :] = jnp.broadcast_to(terms, (8, DH)).astype(BF)

    for head in range(2):

        @pl.when(core_ref[0] == head)
        def _():
            fill(mine_ref, head)
            fill(other_ref, 1 - head)

        tiles = []
        for ref in (gate_ref, up_ref):
            wide = ref[head].astype(F32)
            tiles += [wide[:, :DH], wide[:, DH:]]
        tiles.append(down_ref[head].astype(F32))
        piece = jnp.concatenate(tiles, 0).astype(BF)
        for row in range(4):
            deal_ref[row, 24 * head : 24 * head + 24, :] = piece


def regroup_kernel(rows_ref, deal_ref):
    for head in range(2):
        for row in range(4):
            piece = rows_ref[row, 24 * head : 24 * head + 24, :]
            for depth in range(8):
                deal_ref[2 * depth + head, 24 * row : 24 * row + 24, :] = piece


def arrange_kernel(core_ref, mine_ref, arrived_ref, own_ref, context_ref, pool_ref):
    own_ref[core_ref[0]] = mine_ref[...]
    own_ref[1 - core_ref[0]] = arrived_ref[...]
    for source in range(2):
        context_ref[source] = own_ref[source, 128:384, :]
        for index in range(2):
            first = 128 * index + 64 * source
            rows = slice(128 * (index + 1), 128 * (index + 1) + 64)
            pool_ref[first : first + 64, :] = own_ref[source, rows, :]
        pool_ref[256 + 8 * source : 264 + 8 * source, :] = own_ref[source, 384:392, :]


def grad_kernel(row_ref, p0_ref, p1_ref, p2_ref, p3_ref, raw_ref, grad_ref, slices_ref, down_ref):
    pools = (p0_ref, p1_ref, p2_ref, p3_ref)
    out_row = lax.broadcasted_iota(jnp.int32, (DH, 2 * DH), 0)
    in_row = lax.broadcasted_iota(jnp.int32, (DH, 2 * DH), 1)
    sender = out_row // 4
    pick = (sender % 16) * 32 + (sender // 16) * 8 + out_row % 4
    for index in range(2):
        first = 8 * index
        pieces = [raw_ref[:, 24 * y + first : 24 * y + first + 8, :].astype(F32) for y in range(4)]
        mixed = jnp.stack(pieces, 1).reshape(2 * DH, DH).astype(BF)
        rows = slice(index * DH, (index + 1) * DH)
        for half in range(2):
            chosen = jnp.where(in_row == pick + 4 * half, 1.0, 0.0).astype(BF)
            ordered = matmul(chosen, mixed).astype(BF)
            slices_ref[2 * half, rows, :] = ordered[:, :PART]
            slices_ref[2 * half + 1, rows, :] = ordered[:, PART:]
    for y in range(4):
        piece = raw_ref[:, 24 * y + 16 : 24 * y + 24, :].astype(F32).reshape(PART, DH)
        down_ref[PART * y : PART * (y + 1), :] = piece.astype(BF)
    row = row_ref[0]
    weights = (slices_ref[row, :DH, :], slices_ref[row, DH:, :])
    down_part = down_ref[pl.ds(pl.multiple_of(row * PART, PART), PART), :]
    equal = lax.broadcasted_iota(jnp.int32, (64, 64), 0) == lax.broadcasted_iota(
        jnp.int32, (64, 64), 1
    )
    columns = []
    for pool in pools:
        for source in range(2):
            terms = pool[256 + 8 * source : 264 + 8 * source, :].astype(F32)[0:1]
            rate = terms[:, 0:64] + (terms[:, 64:128] + terms[:, 128:192])
            spread = jnp.where(equal, jnp.broadcast_to(rate, (64, 64)), 0.0)
            columns.append(jnp.sum(spread, axis=1, keepdims=True))
    rate_col = jnp.concatenate(columns, 0)
    gate_part, up_part = weights
    keys_now = rms_norm(jnp.concatenate([pool[0:128, :] for pool in pools], 0))
    vals_now = jnp.concatenate([pool[128:256, :] for pool in pools], 0)
    gate_pre = matmul(keys_now, gate_part)
    up_pre = matmul(keys_now, up_part)
    back = matmul_nt(vals_now, down_part)
    sigmoid_val = sigmoid(gate_pre)
    act_val = gate_pre * sigmoid_val
    rate_back = rate_col * back
    d_gate = (rate_back * up_pre * sigmoid_val * (1.0 + gate_pre * (1.0 - sigmoid_val))).astype(BF)
    d_up = (rate_back * act_val).astype(BF)
    h_rate = (rate_col * act_val * up_pre).astype(BF)
    for index, (left, right) in enumerate(
        ((keys_now, d_gate), (keys_now, d_up), (vals_now, h_rate))
    ):
        grad = matmul_tn(left, right).reshape(8, 32, PART)
        grad_ref[:, index * 32 : index * 32 + 32, :] = grad.astype(BF)


def sum_kernel(parts_ref, total_ref):
    total = jnp.sum(parts_ref[...].astype(F32), axis=0, keepdims=True)
    total_ref[...] = jnp.broadcast_to(total, (CHIPS, 96, PART)).astype(BF)


def whole_weights(slices_ref):
    gate_fast = jnp.concatenate([slices_ref[row, :DH, :] for row in range(4)], 1)
    up_fast = jnp.concatenate([slices_ref[row, DH:, :] for row in range(4)], 1)
    return gate_fast, up_fast


def attention_kernel(
    chip_ref, own_ref, c1_ref, c2_ref, c3_ref, c4_ref, slices_ref, down_ref, out_ref
):
    chip = chip_ref[0]
    row = lax.broadcasted_iota(jnp.int32, (TOK, TOK), 0)
    column = lax.broadcasted_iota(jnp.int32, (TOK, TOK), 1)
    scale = 1.0 / math.sqrt(DH)
    chunks = (c1_ref, c2_ref, c3_ref, c4_ref)

    def rows_of(distance, index, block):
        if distance == 0:
            first = (2 + 2 * index + block) * 64
            return jnp.concatenate([own_ref[src, first : first + 64, :] for src in range(2)], 0)
        behind = (chip < distance).astype(jnp.int32)
        place = 2 * index + jnp.maximum(block - behind, 0)
        chunk = chunks[distance - 1]
        return jnp.concatenate([chunk[0, place], chunk[1, place]], 0)

    for block in range(2):
        rows = slice(block * 64, block * 64 + 64)
        query = jnp.concatenate([own_ref[0, rows, :], own_ref[1, rows, :]], 0)
        scores = []
        for distance in range(REACH + 1):
            score = matmul_nt(query, rows_of(distance, 0, block)) * scale
            if distance == 0:
                score = jnp.where(row >= column, score, -1e30)
            elif distance == REACH:
                score = jnp.where(row < column, score, -1e30)
            if block == 0 and distance > 0:
                behind = (chip < distance).astype(jnp.int32)
                score = jnp.where(behind + jnp.zeros_like(row) > 0, -1e30, score)
            scores.append(score)
        top = scores[0]
        for score in scores[1:]:
            top = jnp.maximum(top, score)
        row_top = jnp.max(top, axis=-1, keepdims=True)
        exps = [jnp.exp(score - row_top) for score in scores]
        total = exps[0]
        for exp_score in exps[1:]:
            total = total + exp_score
        row_sum = jnp.sum(total, axis=-1, keepdims=True)
        result = None
        for distance in range(REACH + 1):
            weights = (exps[distance] / row_sum).astype(BF)
            part = matmul(weights, rows_of(distance, 1, block))
            result = part if result is None else result + part
        if block == 0:
            result = result + fast_forward(query, *whole_weights(slices_ref), down_ref[...])
        out_ref[block] = result


def coarse_step(iterates):
    highs = [iterate.astype(BF) for iterate in iterates]
    grams = [matmul_nt(high, high) for high in highs]
    squares = [matmul(gram.astype(BF), gram.astype(BF)) for gram in grams]
    polys = [-4.775 * gram + 2.0315 * square for gram, square in zip(grams, squares)]
    changes = [matmul(poly.astype(BF), high) for poly, high in zip(polys, highs)]
    return [3.4445 * iterate + change for iterate, change in zip(iterates, changes)]


def thrice(left, right, axis):
    left = jnp.concatenate([left[0], left[0], left[1]], 1)
    return left, jnp.concatenate([right[0], right[1], right[0]], axis)


def fine_step(iterates):
    parts = [halves(iterate) for iterate in iterates]
    grams = [matmul_nt(*thrice(part, part, 1)) for part in parts]
    gram_parts = [halves(gram) for gram in grams]
    squares = [matmul(*thrice(part, part, 0)) for part in gram_parts]
    polys = [halves(-4.775 * gram + 2.0315 * square) for gram, square in zip(grams, squares)]
    changes = [matmul(*thrice(poly, part, 0)) for poly, part in zip(polys, parts)]
    return [3.4445 * iterate + change for iterate, change in zip(iterates, changes)]


def newton_kernel(
    step_ref, total_ref, slices_ref, down_ref, own_ref, base_ref, out_ref, iterate_ref
):
    for index in range(3):
        rows = slice(index * 32, index * 32 + 32)
        pieces = [total_ref[row, :, rows, :].astype(F32).reshape(DH, PART) for row in range(4)]
        grad = jnp.concatenate(pieces, 1)
        square = jnp.sum(jnp.sum(grad * grad, axis=0, keepdims=True), axis=1, keepdims=True)
        iterate_ref[index] = grad / (jnp.sqrt(square) + 1e-07)

    iterates = [iterate_ref[index] for index in range(3)]
    for step_index in range(NS_STEPS):
        iterates = coarse_step(iterates) if step_index < 2 else fine_step(iterates)
        for index in range(3):
            iterate_ref[index] = iterates[index]
        iterates = [iterate_ref[index] for index in range(3)]
    step = step_ref[0]
    gate_fast, up_fast = whole_weights(slices_ref)
    gate_fast = (gate_fast.astype(F32) + step * iterate_ref[0]).astype(BF)
    up_fast = (up_fast.astype(F32) + step * iterate_ref[1]).astype(BF)
    down_fast = (down_ref[...].astype(F32) + step * iterate_ref[2].T).astype(BF)
    query = jnp.concatenate([own_ref[0, 64:128, :], own_ref[1, 64:128, :]], 0)
    fast = fast_forward(query, gate_fast, up_fast, down_fast)
    out_ref[:, 0] = base_ref[0].reshape(16, 8, DH).astype(BF)
    out_ref[:, 1] = (fast + base_ref[1]).reshape(16, 8, DH).astype(BF)


def norm_kernel(parts_ref, gain_ref, out_ref):
    square = None
    for source in range(16):
        wide = parts_ref[source].astype(F32)
        part = jnp.sum(wide * wide, axis=-1, keepdims=True)
        square = part if square is None else square + part
    scale = lax.rsqrt(square * (1.0 / (16 * DH)) + 1e-06)
    for source in range(16):
        head = 2 * (source % 8) + source // 8
        columns = slice(head * DH, (head + 1) * DH)
        wide = parts_ref[source].astype(F32) * scale * gain_ref[:, columns][None]
        out_ref[:, :, columns] = wide.astype(BF)


PARAMS = pltpu.CompilerParams(vmem_limit_bytes=16 * 1024 * 1024)
VMEM = pl.BlockSpec(memory_space=pltpu.VMEM)
ANY = pl.BlockSpec(memory_space=pl.ANY)
HBM = pl.BlockSpec(memory_space=pltpu.HBM)
SMEM = pl.BlockSpec(memory_space=pltpu.SMEM)


def shape_of(shape, dtype=BF):
    return jax.ShapeDtypeStruct(shape, dtype)


def body(queries, keys, values, token_rates, step_size, w_gate, w_up, w_down, norm_gain):
    core = lax.axis_index("core")
    chip = lax.axis_index(RING).astype(jnp.int32).reshape(1)
    line = lax.axis_index("y_hi").astype(jnp.int32).reshape(1)
    pieces = (queries, keys, values, token_rates, w_gate, w_up, w_down)
    place = core.astype(jnp.int32).reshape(1)
    mine, other, dealt = pl.pallas_call(
        pack_kernel,
        out_shape=(shape_of((392, DH)), shape_of((392, DH)), shape_of((4, 48, DH))),
        in_specs=[SMEM] + [HBM] * 7,
        out_specs=(VMEM,) * 3,
        scratch_shapes=[pltpu.VMEM(piece.shape, piece.dtype) for piece in pieces]
        + [pltpu.SemaphoreType.DMA((7,))],
        compiler_params=pltpu.CompilerParams(vmem_limit_bytes=61500 * 1024),
        name="pack",
    )(place, *pieces)
    dealt = lax.all_to_all(dealt, "y_hi", 0, 0, tiled=True)
    dealt = pl.pallas_call(
        regroup_kernel,
        out_shape=shape_of((16, 96, DH)),
        in_specs=[VMEM],
        out_specs=VMEM,
        compiler_params=PARAMS,
        name="regroup",
    )(dealt)
    dealt = lax.all_to_all(dealt, ("z", "core"), 0, 0, tiled=True)
    arrived = lax.ppermute(other, "core", [(0, 1), (1, 0)])
    own, context, pool = pl.pallas_call(
        arrange_kernel,
        out_shape=(shape_of((2, 392, DH)), shape_of((2, 256, DH)), shape_of((272, DH))),
        in_specs=[SMEM, VMEM, VMEM],
        out_specs=(VMEM,) * 3,
        compiler_params=PARAMS,
        name="arrange",
    )(place, mine, arrived)
    pools = [pool]
    for distance in range(1, 4):
        pools.append(lax.ppermute(pool, "y_hi", [(i, (i + distance) % 4) for i in range(4)]))
    ring = [(i, (i + 1) % CHIPS) for i in range(CHIPS)]
    chunks = [lax.ppermute(context, RING, ring)]

    grad, slices, down_fast = pl.pallas_call(
        grad_kernel,
        out_shape=(shape_of((8, 96, PART)), shape_of((4, 2 * DH, PART)), shape_of((DF, DH))),
        in_specs=[SMEM] + [VMEM] * 5,
        out_specs=(VMEM,) * 3,
        compiler_params=PARAMS,
        name="grad",
    )(line, *pools, dealt)
    parts = lax.all_to_all(grad, "z", 0, 0, tiled=True)
    chunks.append(lax.ppermute(chunks[-1], RING, ring))
    total = pl.pallas_call(
        sum_kernel,
        out_shape=shape_of((CHIPS, 96, PART)),
        in_specs=[VMEM],
        out_specs=VMEM,
        compiler_params=PARAMS,
        name="sum",
    )(parts)
    total = lax.all_to_all(total, RING, 0, 0, tiled=True)
    total = total.reshape(4, 8, 96, PART)
    chunks.append(lax.ppermute(chunks[-1], RING, ring))

    chunks.append(lax.ppermute(chunks[-1], RING, ring))
    chunks = [chunk.reshape(2, 4, 64, DH) for chunk in chunks]
    base = pl.pallas_call(
        attention_kernel,
        out_shape=shape_of((2, TOK, DH), F32),
        in_specs=[SMEM] + [VMEM] * 7,
        out_specs=VMEM,
        compiler_params=PARAMS,
        name="window",
    )(chip, own, *chunks, slices, down_fast)
    step = lax.dynamic_slice_in_dim(step_size, core, 1, 0)
    combined = pl.pallas_call(
        newton_kernel,
        out_shape=shape_of((16, 2, 8, DH)),
        in_specs=[SMEM] + [VMEM] * 5,
        out_specs=VMEM,
        scratch_shapes=[pltpu.VMEM((3, DH, DF), F32)],
        compiler_params=PARAMS,
        name="newton",
    )(step, total, slices, down_fast, own, base)
    gathered = lax.all_to_all(combined, ("core", "y_lo", "x"), 0, 0, tiled=True)
    return pl.pallas_call(
        norm_kernel,
        out_shape=jax.ShapeDtypeStruct((2, 8, 16 * DH), BF),
        in_specs=[VMEM] * 2,
        out_specs=VMEM,
        compiler_params=PARAMS,
        name="norm",
    )(gathered, norm_gain.reshape(1, 16 * DH))


def solution(mesh):
    fine = Mesh(mesh.devices.reshape(2, 4, 4, 8, 2), ("y_lo", "x", "y_hi", "z", "core"))
    seq = RING + ("core",)
    head = ("y_lo", "x")
    placed = (
        P(None, seq, head),
        P(None, seq, head),
        P(None, seq, head),
        P(None, head, seq),
        P(head),
        P(head, seq, None),
        P(head, seq, None),
        P(head, seq, None),
        P(),
    )
    return jax.shard_map(
        body, mesh=fine, in_specs=placed, out_specs=P(None, seq + head, None), check_vma=False
    )
```

```python
import math

import jax
import jax.numpy as jnp
from jax import lax
from jax.experimental import pallas as pl
from jax.experimental.pallas import tpu as pltpu
from jax.sharding import Mesh
from jax.sharding import PartitionSpec as P

DH = 256
DF = 512
PART = 128
NS_STEPS = 5
CHIPS = 32
TOK = 128
REACH = 4
RING = ("y_hi", "z")
F32 = jnp.float32
BF = jnp.bfloat16


def matmul(left, right):
    return lax.dot_general(left, right, (((1,), (0,)), ((), ())), preferred_element_type=F32)


def matmul_nt(left, right):
    return lax.dot_general(left, right, (((1,), (1,)), ((), ())), preferred_element_type=F32)


def matmul_tn(left, right):
    return lax.dot_general(left, right, (((0,), (0,)), ((), ())), preferred_element_type=F32)


def halves(wide):
    high = wide.astype(BF)
    return high, (wide - high.astype(F32)).astype(BF)


def rms_norm(values_in):
    wide = values_in.astype(F32)
    mean_square = jnp.mean(wide * wide, axis=-1, keepdims=True)
    return (wide * lax.rsqrt(mean_square + 1e-06)).astype(BF)


def sigmoid(value):
    return 1.0 / (1.0 + jnp.exp(-value))


def fast_forward(query, gate_fast, up_fast, down_fast):
    query_norm = rms_norm(query)
    gate_query = matmul(query_norm, gate_fast)
    up_query = matmul(query_norm, up_fast)
    hidden = (gate_query * sigmoid(gate_query) * up_query).astype(BF)
    return matmul(hidden, down_fast)


def pack_kernel(
    core_ref, q_in, k_in, v_in, rate_in, gate_in, up_in, down_in, mine_ref, other_ref, deal_ref, *scratch
):
    sources = (q_in, k_in, v_in, rate_in, gate_in, up_in, down_in)
    q_ref, k_ref, v_ref, rate_ref, gate_ref, up_ref, down_ref = scratch[:7]
    semaphores = scratch[7]
    copies = [
        pltpu.make_async_copy(source, target, semaphores.at[index])
        for index, (source, target) in enumerate(zip(sources, scratch[:7]))
    ]
    for copy in copies:
        copy.start()
    for copy in copies:
        copy.wait()

    def fill(target, head):
        columns = slice(head * DH, (head + 1) * DH)
        for index, ref in enumerate((q_ref, k_ref, v_ref)):
            for block in range(2):
                first = (index * 2 + block) * 64
                target[first : first + 64, :] = ref[block, :, columns]
        rate = rate_ref[0, head : head + 1, :]
        high = rate.astype(BF).astype(F32)
        middle = (rate - high).astype(BF).astype(F32)
        low = (rate - high) - middle
        terms = jnp.concatenate([high, middle, low, jnp.zeros_like(rate)], 1)
        target[384:392, :] = jnp.broadcast_to(terms, (8, DH)).astype(BF)

    for head in range(2):

        @pl.when(core_ref[0] == head)
        def _():
            fill(mine_ref, head)
            fill(other_ref, 1 - head)

        tiles = []
        for ref in (gate_ref, up_ref):
            wide = ref[head].astype(F32)
            tiles += [wide[:, :DH], wide[:, DH:]]
        tiles.append(down_ref[head].astype(F32))
        piece = jnp.concatenate(tiles, 0).astype(BF)
        for row in range(4):
            deal_ref[row, 24 * head : 24 * head + 24, :] = piece


def regroup_kernel(rows_ref, deal_ref):
    for head in range(2):
        for row in range(4):
            piece = rows_ref[row, 24 * head : 24 * head + 24, :]
            for depth in range(8):
                deal_ref[2 * depth + head, 24 * row : 24 * row + 24, :] = piece


def arrange_kernel(core_ref, mine_ref, arrived_ref, own_ref, context_ref, pool_ref):
    own_ref[core_ref[0]] = mine_ref[...]
    own_ref[1 - core_ref[0]] = arrived_ref[...]
    for source in range(2):
        context_ref[source] = own_ref[source, 128:384, :]
        for index in range(2):
            first = 128 * index + 64 * source
            rows = slice(128 * (index + 1), 128 * (index + 1) + 64)
            pool_ref[first : first + 64, :] = own_ref[source, rows, :]
        pool_ref[256 + 8 * source : 264 + 8 * source, :] = own_ref[source, 384:392, :]


def grad_kernel(row_ref, p0_ref, p1_ref, p2_ref, p3_ref, raw_ref, grad_ref, slices_ref, down_ref):
    pools = (p0_ref, p1_ref, p2_ref, p3_ref)
    out_row = lax.broadcasted_iota(jnp.int32, (DH, 2 * DH), 0)
    in_row = lax.broadcasted_iota(jnp.int32, (DH, 2 * DH), 1)
    sender = out_row // 4
    pick = (sender % 16) * 32 + (sender // 16) * 8 + out_row % 4
    for index in range(2):
        first = 8 * index
        pieces = [raw_ref[:, 24 * y + first : 24 * y + first + 8, :].astype(F32) for y in range(4)]
        mixed = jnp.stack(pieces, 1).reshape(2 * DH, DH).astype(BF)
        rows = slice(index * DH, (index + 1) * DH)
        for half in range(2):
            chosen = jnp.where(in_row == pick + 4 * half, 1.0, 0.0).astype(BF)
            ordered = matmul(chosen, mixed).astype(BF)
            slices_ref[2 * half, rows, :] = ordered[:, :PART]
            slices_ref[2 * half + 1, rows, :] = ordered[:, PART:]
    for y in range(4):
        piece = raw_ref[:, 24 * y + 16 : 24 * y + 24, :].astype(F32).reshape(PART, DH)
        down_ref[PART * y : PART * (y + 1), :] = piece.astype(BF)
    row = row_ref[0]
    weights = (slices_ref[row, :DH, :], slices_ref[row, DH:, :])
    down_part = down_ref[pl.ds(pl.multiple_of(row * PART, PART), PART), :]
    equal = lax.broadcasted_iota(jnp.int32, (64, 64), 0) == lax.broadcasted_iota(
        jnp.int32, (64, 64), 1
    )
    columns = []
    for pool in pools:
        for source in range(2):
            terms = pool[256 + 8 * source : 264 + 8 * source, :].astype(F32)[0:1]
            rate = terms[:, 0:64] + (terms[:, 64:128] + terms[:, 128:192])
            spread = jnp.where(equal, jnp.broadcast_to(rate, (64, 64)), 0.0)
            columns.append(jnp.sum(spread, axis=1, keepdims=True))
    rate_col = jnp.concatenate(columns, 0)
    gate_part, up_part = weights
    keys_now = rms_norm(jnp.concatenate([pool[0:128, :] for pool in pools], 0))
    vals_now = jnp.concatenate([pool[128:256, :] for pool in pools], 0)
    gate_pre = matmul(keys_now, gate_part)
    up_pre = matmul(keys_now, up_part)
    back = matmul_nt(vals_now, down_part)
    sigmoid_val = sigmoid(gate_pre)
    act_val = gate_pre * sigmoid_val
    rate_back = rate_col * back
    d_gate = (rate_back * up_pre * sigmoid_val * (1.0 + gate_pre * (1.0 - sigmoid_val))).astype(BF)
    d_up = (rate_back * act_val).astype(BF)
    h_rate = (rate_col * act_val * up_pre).astype(BF)
    for index, (left, right) in enumerate(
        ((keys_now, d_gate), (keys_now, d_up), (vals_now, h_rate))
    ):
        grad = matmul_tn(left, right).reshape(8, 32, PART)
        grad_ref[:, index * 32 : index * 32 + 32, :] = grad.astype(BF)


def sum_kernel(parts_ref, total_ref):
    total = jnp.sum(parts_ref[...].astype(F32), axis=0, keepdims=True)
    total_ref[...] = jnp.broadcast_to(total, (CHIPS, 96, PART)).astype(BF)


def whole_weights(slices_ref):
    gate_fast = jnp.concatenate([slices_ref[row, :DH, :] for row in range(4)], 1)
    up_fast = jnp.concatenate([slices_ref[row, DH:, :] for row in range(4)], 1)
    return gate_fast, up_fast


def attention_kernel(
    chip_ref, own_ref, c1_ref, c2_ref, c3_ref, c4_ref, slices_ref, down_ref, fast_ref, out_ref
):
    chip = chip_ref[0]
    row = lax.broadcasted_iota(jnp.int32, (TOK, TOK), 0)
    column = lax.broadcasted_iota(jnp.int32, (TOK, TOK), 1)
    scale = 1.0 / math.sqrt(DH)
    chunks = (c1_ref, c2_ref, c3_ref, c4_ref)

    def rows_of(distance, index, block):
        if distance == 0:
            first = (2 + 2 * index + block) * 64
            return jnp.concatenate([own_ref[src, first : first + 64, :] for src in range(2)], 0)
        behind = (chip < distance).astype(jnp.int32)
        place = 2 * index + jnp.maximum(block - behind, 0)
        chunk = chunks[distance - 1]
        return jnp.concatenate([chunk[0, place], chunk[1, place]], 0)

    for block in range(2):
        rows = slice(block * 64, block * 64 + 64)
        query = jnp.concatenate([own_ref[0, rows, :], own_ref[1, rows, :]], 0)
        scores = []
        for distance in range(REACH + 1):
            score = matmul_nt(query, rows_of(distance, 0, block)) * scale
            if distance == 0:
                score = jnp.where(row >= column, score, -1e30)
            elif distance == REACH:
                score = jnp.where(row < column, score, -1e30)
            if block == 0 and distance > 0:
                behind = (chip < distance).astype(jnp.int32)
                score = jnp.where(behind + jnp.zeros_like(row) > 0, -1e30, score)
            scores.append(score)
        top = scores[0]
        for score in scores[1:]:
            top = jnp.maximum(top, score)
        row_top = jnp.max(top, axis=-1, keepdims=True)
        exps = [jnp.exp(score - row_top) for score in scores]
        total = exps[0]
        for exp_score in exps[1:]:
            total = total + exp_score
        row_sum = jnp.sum(total, axis=-1, keepdims=True)
        result = None
        for distance in range(REACH + 1):
            weights = (exps[distance] / row_sum).astype(BF)
            part = matmul(weights, rows_of(distance, 1, block))
            result = part if result is None else result + part
        if block == 0:
            result = result + fast_forward(query, *whole_weights(slices_ref), down_ref[...])
        else:
            result = result + fast_ref[...]
        out_ref[:, block] = result.reshape(16, 8, DH).astype(BF)


def coarse_step(iterates):
    highs = [iterate.astype(BF) for iterate in iterates]
    grams = [matmul_nt(high, high) for high in highs]
    squares = [matmul(gram.astype(BF), gram.astype(BF)) for gram in grams]
    polys = [-4.775 * gram + 2.0315 * square for gram, square in zip(grams, squares)]
    changes = [matmul(poly.astype(BF), high) for poly, high in zip(polys, highs)]
    return [3.4445 * iterate + change for iterate, change in zip(iterates, changes)]


def thrice(left, right, axis):
    left = jnp.concatenate([left[0], left[0], left[1]], 1)
    return left, jnp.concatenate([right[0], right[1], right[0]], axis)


def fine_step(iterates):
    parts = [halves(iterate) for iterate in iterates]
    grams = [matmul_nt(*thrice(part, part, 1)) for part in parts]
    gram_parts = [halves(gram) for gram in grams]
    squares = [matmul(*thrice(part, part, 0)) for part in gram_parts]
    polys = [halves(-4.775 * gram + 2.0315 * square) for gram, square in zip(grams, squares)]
    changes = [matmul(*thrice(poly, part, 0)) for poly, part in zip(polys, parts)]
    return [3.4445 * iterate + change for iterate, change in zip(iterates, changes)]


def newton_kernel(
    step_ref, total_ref, slices_ref, down_ref, own_ref, _, fast_ref, iterate_ref
):
    for index in range(3):
        rows = slice(index * 32, index * 32 + 32)
        pieces = [total_ref[row, :, rows, :].astype(F32).reshape(DH, PART) for row in range(4)]
        grad = jnp.concatenate(pieces, 1)
        square = jnp.sum(jnp.sum(grad * grad, axis=0, keepdims=True), axis=1, keepdims=True)
        iterate_ref[index] = grad / (jnp.sqrt(square) + 1e-07)

    iterates = [iterate_ref[index] for index in range(3)]
    for step_index in range(NS_STEPS):
        iterates = coarse_step(iterates) if step_index < 2 else fine_step(iterates)
        for index in range(3):
            iterate_ref[index] = iterates[index]
        iterates = [iterate_ref[index] for index in range(3)]
    step = step_ref[0]
    gate_fast, up_fast = whole_weights(slices_ref)
    gate_fast = (gate_fast.astype(F32) + step * iterate_ref[0]).astype(BF)
    up_fast = (up_fast.astype(F32) + step * iterate_ref[1]).astype(BF)
    down_fast = (down_ref[...].astype(F32) + step * iterate_ref[2].T).astype(BF)
    query = jnp.concatenate([own_ref[0, 64:128, :], own_ref[1, 64:128, :]], 0)
    fast_ref[...] = fast_forward(query, gate_fast, up_fast, down_fast)


def norm_kernel(parts_ref, gain_ref, out_ref):
    square = None
    for source in range(16):
        wide = parts_ref[source].astype(F32)
        part = jnp.sum(wide * wide, axis=-1, keepdims=True)
        square = part if square is None else square + part
    scale = lax.rsqrt(square * (1.0 / (16 * DH)) + 1e-06)
    for source in range(16):
        head = 2 * (source % 8) + source // 8
        columns = slice(head * DH, (head + 1) * DH)
        wide = parts_ref[source].astype(F32) * scale * gain_ref[:, columns][None]
        out_ref[:, :, columns] = wide.astype(BF)


PARAMS = pltpu.CompilerParams(vmem_limit_bytes=16 * 1024 * 1024)
VMEM = pl.BlockSpec(memory_space=pltpu.VMEM)
ANY = pl.BlockSpec(memory_space=pl.ANY)
HBM = pl.BlockSpec(memory_space=pltpu.HBM)
SMEM = pl.BlockSpec(memory_space=pltpu.SMEM)


def shape_of(shape, dtype=BF):
    return jax.ShapeDtypeStruct(shape, dtype)


def body(queries, keys, values, token_rates, step_size, w_gate, w_up, w_down, norm_gain):
    core = lax.axis_index("core")
    chip = lax.axis_index(RING).astype(jnp.int32).reshape(1)
    line = lax.axis_index("y_hi").astype(jnp.int32).reshape(1)
    pieces = (queries, keys, values, token_rates, w_gate, w_up, w_down)
    place = core.astype(jnp.int32).reshape(1)
    mine, other, dealt = pl.pallas_call(
        pack_kernel,
        out_shape=(shape_of((392, DH)), shape_of((392, DH)), shape_of((4, 48, DH))),
        in_specs=[SMEM] + [HBM] * 7,
        out_specs=(VMEM,) * 3,
        scratch_shapes=[pltpu.VMEM(piece.shape, piece.dtype) for piece in pieces]
        + [pltpu.SemaphoreType.DMA((7,))],
        compiler_params=pltpu.CompilerParams(vmem_limit_bytes=61500 * 1024),
        name="pack",
    )(place, *pieces)
    dealt = lax.all_to_all(dealt, "y_hi", 0, 0, tiled=True)
    dealt = pl.pallas_call(
        regroup_kernel,
        out_shape=shape_of((16, 96, DH)),
        in_specs=[VMEM],
        out_specs=VMEM,
        compiler_params=PARAMS,
        name="regroup",
    )(dealt)
    dealt = lax.all_to_all(dealt, ("z", "core"), 0, 0, tiled=True)
    arrived = lax.ppermute(other, "core", [(0, 1), (1, 0)])
    own, context, pool = pl.pallas_call(
        arrange_kernel,
        out_shape=(shape_of((2, 392, DH)), shape_of((2, 256, DH)), shape_of((272, DH))),
        in_specs=[SMEM, VMEM, VMEM],
        out_specs=(VMEM,) * 3,
        compiler_params=PARAMS,
        name="arrange",
    )(place, mine, arrived)
    pools = [pool]
    for distance in range(1, 4):
        pools.append(lax.ppermute(pool, "y_hi", [(i, (i + distance) % 4) for i in range(4)]))
    ring = [(i, (i + 1) % CHIPS) for i in range(CHIPS)]
    chunks = [lax.ppermute(context, RING, ring)]

    grad, slices, down_fast = pl.pallas_call(
        grad_kernel,
        out_shape=(shape_of((8, 96, PART)), shape_of((4, 2 * DH, PART)), shape_of((DF, DH))),
        in_specs=[SMEM] + [VMEM] * 5,
        out_specs=(VMEM,) * 3,
        compiler_params=PARAMS,
        name="grad",
    )(line, *pools, dealt)
    parts = lax.all_to_all(grad, "z", 0, 0, tiled=True)
    chunks.append(lax.ppermute(chunks[-1], RING, ring))
    total = pl.pallas_call(
        sum_kernel,
        out_shape=shape_of((CHIPS, 96, PART)),
        in_specs=[VMEM],
        out_specs=VMEM,
        compiler_params=PARAMS,
        name="sum",
    )(parts)
    chunks.append(lax.ppermute(chunks[-1], RING, ring))
    total = lax.all_to_all(total, RING, 0, 0, tiled=True)
    total = total.reshape(4, 8, 96, PART)

    step = lax.dynamic_slice_in_dim(step_size, core, 1, 0)
    fast = pl.pallas_call(
        newton_kernel,
        out_shape=shape_of((TOK, DH), F32),
        in_specs=[SMEM] + [VMEM] * 4 + [ANY],
        out_specs=VMEM,
        scratch_shapes=[pltpu.VMEM((3, DH, DF), F32)],
        compiler_params=PARAMS,
        cost_estimate=pl.CostEstimate(
            flops=8_000_000_000, transcendentals=100_000, bytes_accessed=4_000_000
        ),
        name="newton",
    )(step, total, slices, down_fast, own, chunks[2])
    chunks.append(lax.ppermute(chunks[-1], RING, ring))
    chunks = [chunk.reshape(2, 4, 64, DH) for chunk in chunks]
    combined = pl.pallas_call(
        attention_kernel,
        out_shape=shape_of((16, 2, 8, DH)),
        in_specs=[SMEM] + [VMEM] * 8,
        out_specs=VMEM,
        compiler_params=PARAMS,
        name="window",
    )(chip, own, *chunks, slices, down_fast, fast)
    gathered = lax.all_to_all(combined, ("core", "y_lo", "x"), 0, 0, tiled=True)
    return pl.pallas_call(
        norm_kernel,
        out_shape=jax.ShapeDtypeStruct((2, 8, 16 * DH), BF),
        in_specs=[VMEM] * 2,
        out_specs=VMEM,
        compiler_params=PARAMS,
        name="norm",
    )(gathered, norm_gain.reshape(1, 16 * DH))


def solution(mesh):
    fine = Mesh(mesh.devices.reshape(2, 4, 4, 8, 2), ("y_lo", "x", "y_hi", "z", "core"))
    seq = RING + ("core",)
    head = ("y_lo", "x")
    placed = (
        P(None, seq, head),
        P(None, seq, head),
        P(None, seq, head),
        P(None, head, seq),
        P(head),
        P(head, seq, None),
        P(head, seq, None),
        P(head, seq, None),
        P(),
    )
    return jax.shard_map(
        body, mesh=fine, in_specs=placed, out_specs=P(None, seq + head, None), check_vma=False
    )
```
